1024 devices in a mesh: batch: 32 (over x_lo, z, core), mem: 32 (over x_hi, y).
Axes of the slice: x: 8 (x_hi: 4, x_lo: 2; x = x_hi * 2 + x_lo), y: 8, z: 8, core: 2. Of those that a mesh axis runs over, the one named last changes fastest.
Arguments:
- queries: bfloat16 [131072, 256], P(('mem', 'batch')), may hold values from -10 to 10
- positives: bfloat16 [131072, 256], P(('mem', 'batch')), may hold values from -0.25 to 0.25, as said below
- pos_ids: int32 [131072], replicated, may hold values from 0 to 31
- pos_logq: int32 [131072], replicated, may hold values from -10240 to -4097
- mem_items: bfloat16 [32768, 256], P(('batch', 'mem')), may hold values from -0.375 to 0.375
- mem_ids: int32 [32768], replicated, may hold values from 0 to 31
- mem_logq: int32 [32768], replicated, may hold values from -12288 to -6145
- mem_age: int32 [32768], replicated, may hold values from 0 to 23
- counts: int32 [16384], replicated, may hold values from 1 to 64, 131072 in all
Outputs:
- row_loss: float32 [131072], P(('mem', 'batch'))
- query_grad: float32 [131072, 256], P(('mem', 'batch'))
- positive_grad: float32 [131072, 256], P(('mem', 'batch'))
The draws below stay inside these ranges and needn't reach their ends.
Inputs may be any that keep to these rules, and one draw needn't show every extreme that they name: `positives`: item embeddings. The counts sum to 131072; the largest is 64.
All inputs are finite; a program needn't handle non-finite values.
Results may differ from the reference program's by a relative error of at most 0.0033.
Values may be sent and summed in bfloat16 or wider, within the bound.
A program may use at most 32 MiB of HBM per device.

```python
import math
import jax
import jax.numpy as jnp
import numpy as np
from jax import lax

D = 256
QB = 128
MEM_DEV = 32
MOST = 64
ITEMS = 32
AGE_LIMIT = 16
IMPS = 131072
MEM_ROWS = 32768
REQS = 16384
N_BATCH = 32
N_MEM = 32


def positive_base(key):
    fresh_draw = jax.random.truncated_normal(jax.random.fold_in(key, 11), -4.0, 4.0, (IMPS, D), jnp.float32) / 16.0
    return fresh_draw


def draw_positives(key, part):
    return positive_base(key).astype(jnp.bfloat16)


def draw_queries(key, part):
    query_noise = jax.random.truncated_normal(jax.random.fold_in(key, 21), -4.0, 4.0, (IMPS, D), jnp.float32) * 0.25
    return query_noise.astype(jnp.bfloat16)


def with_ends(array, stream_key, smallest, top_value):
    longest = array.shape.index(max(array.shape))
    spots = []
    for shift in (0, 1):
        where = [jax.random.randint(jax.random.fold_in(stream_key, axis), (), 0, length) for axis, length in enumerate(array.shape)]
        where[longest] = (where[longest] + shift) % array.shape[longest]
        spots.append(tuple(where))
    return array.at[spots[0]].set(smallest).at[spots[1]].set(top_value)


def steps_of(key, shape, cuts, least, largest):
    level = 1.0
    for axis_at, blocks in cuts:
        steps = jax.random.uniform(jax.random.fold_in(jax.random.fold_in(key, 6), axis_at), (blocks,), jnp.float32, least / len(cuts), largest / len(cuts))
        level = level * jnp.repeat(jnp.exp(steps), shape[axis_at] // blocks).reshape((-1,) + (1,) * (len(shape) - 1 - axis_at))
    return level


def rank_table(count, lean):
    weights = [(1 << 20) // math.isqrt(standing ** lean) + 1 for standing in range(1, count + 1)]
    deviation = 1 + sum(weights) // (1 << 30)
    return np.cumsum(np.array([max(1, weight // deviation) for weight in weights]))


def ranked(stream_key, extent, number_of, lean):
    table = rank_table(number_of, lean)
    lot = jax.random.randint(jax.random.fold_in(stream_key, 1), extent, 0, int(table[number_of - 1]))
    grade = jnp.searchsorted(jnp.asarray(table, jnp.int32), lot, side="right")
    return jax.random.permutation(jax.random.fold_in(stream_key, 2), number_of)[grade].astype(jnp.int32)


def split_up(count, total, limit, lean):
    weights = [(1 << 20) // math.isqrt(standing ** lean) + 1 for standing in range(2, count + 1)]
    spare, holding = total - limit - (count - 1), [1] * (count - 1)
    while spare > 0:
        free = [i for i in range(count - 1) if holding[i] < limit]
        pool, budget = sum([weights[i] for i in free]), spare
        for i in free:
            extra = min(limit - holding[i], max(1, budget * weights[i] // pool), spare)
            holding[i] = holding[i] + extra
            spare = spare - extra
    return np.array([limit] + holding)


def ragged_sizes(rng, number_of, total, most, skew):
    if number_of == 2:
        one = jax.random.randint(rng, (), max(1, total - most), min(most, total - 1) + 1)
        return jnp.stack([one, total - one])
    tallies = jnp.asarray(split_up(number_of, total, most, skew), jnp.int32)
    couples = (number_of - 1) // 2
    donor, sink = tallies[1:1 + 2 * couples:2], tallies[2:2 + 2 * couples:2]
    margin = jnp.minimum(donor - 1, most - sink)
    shifted = jax.random.randint(jax.random.fold_in(rng, 1), (couples,), 0, 1 << 20) % (margin + 1)
    tallies = tallies.at[1:1 + 2 * couples:2].set(donor - shifted).at[2:2 + 2 * couples:2].set(sink + shifted)
    return tallies[jax.random.permutation(jax.random.fold_in(rng, 2), number_of)]


def centred(own_key, shape, scale, limit, pieces=(), kind=jnp.bfloat16):
    drawn = scale * jax.random.normal(own_key, shape, jnp.float32)
    if pieces:
        drawn = drawn * steps_of(own_key, shape, pieces, -0.22, 0.18)
    return jnp.clip(drawn, -limit, limit).astype(kind)


def setup_inputs(seed: int = 0) -> dict:
    key_of = jax.random.split(jax.random.key(seed), 10)
    return {
        "queries": draw_queries(jax.random.fold_in(key_of[9], 71), 0),
        "positives": draw_positives(jax.random.fold_in(key_of[9], 71), 0),
        "pos_ids": with_ends(ranked(key_of[2], (IMPS,), ITEMS, 2), jax.random.fold_in(key_of[2], 3), 0, ITEMS - 1).astype(jnp.int32),
        "pos_logq": with_ends(jax.random.randint(key_of[3], (IMPS,), -10240, -4096), jax.random.fold_in(key_of[3], 1), -10240, (-4096) - 1).astype(jnp.int32),
        "mem_items": centred(key_of[4], (MEM_ROWS, D), 0.0625, 0.375, ((0, 1024),)),
        "mem_ids": with_ends(ranked(key_of[5], (MEM_ROWS,), ITEMS, 2), jax.random.fold_in(key_of[5], 3), 0, ITEMS - 1).astype(jnp.int32),
        "mem_logq": with_ends(jax.random.randint(key_of[6], (MEM_ROWS,), -12288, -6144), jax.random.fold_in(key_of[6], 1), -12288, (-6144) - 1).astype(jnp.int32),
        "mem_age": with_ends(jax.random.randint(key_of[7], (MEM_ROWS,), 0, 24), jax.random.fold_in(key_of[7], 1), 0, 23).astype(jnp.int32),
        "counts": ragged_sizes(key_of[8], REQS, IMPS, MOST, 2).astype(jnp.int32),
    }


inv_temp = 8.0
logq_unit = 1.0 / 1024.0


def request_of(counts, positions):
    req_ends = jnp.cumsum(counts)
    return jnp.searchsorted(req_ends, positions, side="right").astype(jnp.int32)


def scores(left_mat, right_mat):
    return lax.dot_general(left_mat, right_mat, (((1,), (1,)), ((), ())), preferred_element_type=jnp.float32)


def reference(queries, positives, pos_ids, pos_logq, mem_items, mem_ids, mem_logq, mem_age, counts):
    group_rows = QB * N_BATCH
    bank_rows = MEM_DEV * N_MEM
    row_index = jnp.arange(IMPS, dtype=jnp.int32)
    request = request_of(counts, row_index)
    weight = 1.0 / jnp.take(counts, request).astype(jnp.float32)
    pos_shift = -pos_logq.astype(jnp.float32) * logq_unit
    mem_shift = -mem_logq.astype(jnp.float32) * logq_unit
    mem_live = mem_age < AGE_LIMIT

    def one_block(grad_total, block_num):
        offset = block_num * QB
        group_first = (offset // group_rows) * group_rows
        bank_first = ((offset % group_rows) // QB) * bank_rows
        query_blk = lax.dynamic_slice_in_dim(queries, offset, QB, 0)
        own_rows = offset + jnp.arange(QB, dtype=jnp.int32)
        own_ids = lax.dynamic_slice_in_dim(pos_ids, offset, QB, 0)
        own_req = lax.dynamic_slice_in_dim(request, offset, QB, 0)
        own_weight = lax.dynamic_slice_in_dim(weight, offset, QB, 0)
        own_pos = lax.dynamic_slice_in_dim(positives, offset, QB, 0)
        own_shift = lax.dynamic_slice_in_dim(pos_shift, offset, QB, 0)
        cand_pos = lax.dynamic_slice_in_dim(positives, group_first, group_rows, 0)
        cand_rows = group_first + jnp.arange(group_rows, dtype=jnp.int32)
        cand_ids = lax.dynamic_slice_in_dim(pos_ids, group_first, group_rows, 0)
        cand_req = lax.dynamic_slice_in_dim(request, group_first, group_rows, 0)
        cand_shift = lax.dynamic_slice_in_dim(pos_shift, group_first, group_rows, 0)
        bank_items = lax.dynamic_slice_in_dim(mem_items, bank_first, bank_rows, 0)
        bank_ids = lax.dynamic_slice_in_dim(mem_ids, bank_first, bank_rows, 0)
        bank_shift = lax.dynamic_slice_in_dim(mem_shift, bank_first, bank_rows, 0)
        bank_live = lax.dynamic_slice_in_dim(mem_live, bank_first, bank_rows, 0)
        diagonal = cand_rows[None, :] == own_rows[:, None]
        keep_pos = diagonal | ((cand_ids[None, :] != own_ids[:, None]) & (cand_req[None, :] != own_req[:, None]))
        keep_mem = bank_live[None, :] & (bank_ids[None, :] != own_ids[:, None])
        pos_logit = inv_temp * scores(query_blk, cand_pos) + cand_shift[None, :]
        mem_logit = inv_temp * scores(query_blk, bank_items) + bank_shift[None, :]
        row_max = jnp.maximum(jnp.max(jnp.where(keep_pos, pos_logit, -jnp.inf), axis=1), jnp.max(jnp.where(keep_mem, mem_logit, -jnp.inf), axis=1))
        pos_exps = jnp.where(keep_pos, jnp.exp(jnp.where(keep_pos, pos_logit, row_max[:, None]) - row_max[:, None]), 0.0)
        mem_exps = jnp.where(keep_mem, jnp.exp(jnp.where(keep_mem, mem_logit, row_max[:, None]) - row_max[:, None]), 0.0)
        row_lse = row_max + jnp.log(jnp.sum(pos_exps, axis=1) + jnp.sum(mem_exps, axis=1))
        pos_prob = jnp.where(keep_pos, jnp.exp(jnp.where(keep_pos, pos_logit, row_lse[:, None]) - row_lse[:, None]), 0.0)
        mem_prob = jnp.where(keep_mem, jnp.exp(jnp.where(keep_mem, mem_logit, row_lse[:, None]) - row_lse[:, None]), 0.0)
        pos_coef = (own_weight[:, None] * pos_prob).astype(jnp.bfloat16)
        mem_coef = (own_weight[:, None] * mem_prob).astype(jnp.bfloat16)
        query_grad = inv_temp * (jnp.dot(pos_coef, cand_pos, preferred_element_type=jnp.float32) + jnp.dot(mem_coef, bank_items, preferred_element_type=jnp.float32)) - inv_temp * own_weight[:, None] * own_pos.astype(jnp.float32)
        column = inv_temp * lax.dot_general(pos_coef, query_blk, (((0,), (0,)), ((), ())), preferred_element_type=jnp.float32)
        current = lax.dynamic_slice_in_dim(grad_total, group_first, group_rows, 0)
        grad_total = lax.dynamic_update_slice_in_dim(grad_total, current + column, group_first, 0)
        own_logit = inv_temp * jnp.sum(query_blk.astype(jnp.float32) * own_pos.astype(jnp.float32), axis=1) + own_shift
        return grad_total, (row_lse - own_logit, query_grad)

    grad_start = jnp.zeros((IMPS, D), jnp.float32)
    pos_grad, (loss_blocks, query_blocks) = lax.scan(one_block, grad_start, jnp.arange(IMPS // QB, dtype=jnp.int32))
    positive_grad = pos_grad - inv_temp * weight[:, None] * queries.astype(jnp.float32)
    return loss_blocks.reshape(IMPS), query_blocks.reshape(IMPS, D), positive_grad
```

```python
import jax
import jax.numpy as jnp
from jax import lax
from jax.experimental import pallas as pl
from jax.experimental.pallas import tpu as pltpu
from jax.sharding import PartitionSpec as P

MESH = pl.DeviceIdType.MESH
AGE_LIMIT = 16
NZ, NY, NH = 8, 8, 4
ROWS, DIM, HALF = 128, 256, 64
BLOCKS = 32
GROUP = ROWS * BLOCKS
SLOTS = 32
BANK = 1024
WINDOW = 34
TEMP = 8.0
UNIT = 1.0 / 1024.0
NEG = -1e30
FLOOR = -1e20
SEMS = 192
BF, F32 = jnp.bfloat16, jnp.float32


def nt(left, right):
    return lax.dot_general(left, right, (((1,), (1,)), ((), ())), preferred_element_type=F32)


def nn(left, right):
    return lax.dot_general(left, right, (((1,), (0,)), ((), ())), preferred_element_type=F32)


def iota(shape, dim):
    return lax.broadcasted_iota(jnp.int32, shape, dim)


def as_rows(row):
    return jnp.broadcast_to(row, (ROWS, ROWS)).T


def as_row(column):
    return jnp.broadcast_to(column, (ROWS, ROWS)).T[0:1, :]


def kernel(
    q_hbm, p_hbm, items_hbm, counts_hbm, ids_hbm, logq_hbm, bids_hbm, blogq_hbm, bage_hbm,
    loss_out, qgrad_out, pgrad_out,
    q_all, p_all, q_chip, p_chip, bank,
    s_ref, t_ref, e_ref, mx_ref,
    counts_v, ids_v, logq_v, bids_v, blogq_v, bage_v,
    hi_ref, lo_ref, dd_ref, idf, reqf, shf, wf, id_c, req_c, sh_c,
    stat_out, stat_in, lse_all, half_out, half_in, col_out, col_in, q_acc, p_acc,
    sm_ref, em_ref,
    send_sems, recv_sems, local_sems,
):
    b = lax.axis_index("batch")
    m = lax.axis_index("mem")
    core = lax.rem(b, 2)
    z = lax.rem(lax.div(b, 2), NZ)
    xl = lax.div(b, 2 * NZ)
    y = lax.rem(m, NY)
    xh = lax.div(m, NY)

    def on_batch(x_at, z_at, core_at):
        return {"batch": x_at * (2 * NZ) + z_at * 2 + core_at, "mem": m}

    def on_mem(h_at, y_at):
        return {"batch": b, "mem": h_at * NY + y_at}

    z_next = {1: lax.rem(z + 1, NZ), -1: lax.rem(z + NZ - 1, NZ)}
    y_next = {1: lax.rem(y + 1, NY), -1: lax.rem(y + NY - 1, NY)}
    z_dev = {s: on_batch(xl, z_next[s], core) for s in (1, -1)}
    y_dev = {s: on_mem(xh, y_next[s]) for s in (1, -1)}
    x_dev = on_batch(1 - xl, z, core)
    c_dev = on_batch(xl, z, 1 - core)
    h_dev = {e: on_mem(lax.rem(xh + e, NH), y) for e in (1, 2, 3)}

    copies = {}

    def send(key, src, dst, device):
        k = len(copies)
        copy = pltpu.make_async_remote_copy(
            src_ref=src,
            dst_ref=dst,
            send_sem=send_sems.at[k],
            recv_sem=recv_sems.at[k],
            device_id=device,
            device_id_type=MESH,
        )
        copy.start()
        copies[key] = copy

    local = []

    def load(src, dst):
        copy = pltpu.make_async_copy(src, dst, local_sems.at[len(local)])
        copy.start()
        local.append(copy)

    load(counts_hbm, counts_v)
    load(ids_hbm.at[pl.ds(m * BLOCKS, BLOCKS)], ids_v)
    load(logq_hbm.at[pl.ds(m * BLOCKS, BLOCKS)], logq_v)
    load(q_hbm, q_all.at[0])
    load(p_hbm, p_all.at[0])
    load(q_hbm, q_chip.at[0])
    load(p_hbm, p_chip.at[0])
    load(items_hbm, bank.at[m])
    load(bids_hbm.at[pl.ds(b * 8, 8)], bids_v)
    load(blogq_hbm.at[pl.ds(b * 8, 8)], blogq_v)
    load(bage_hbm.at[pl.ds(b * 8, 8)], bage_v)

    barrier = pltpu.get_barrier_semaphore()
    near = [z_dev[1], z_dev[-1], y_dev[1], y_dev[-1], x_dev, c_dev, h_dev[1], h_dev[2], h_dev[3]]
    for device in near:
        pl.semaphore_signal(barrier, inc=1, device_id=device, device_id_type=MESH)
    pl.semaphore_wait(barrier, len(near))

    own = {"q": q_hbm, "p": p_hbm}
    held = {"q": q_all, "p": p_all}
    last = {"p": {1: 4, -1: 3}, "q": {1: 3, -1: 4}}

    def piece(arr, col, h, d):
        rows = pl.ds(h * HALF, HALF)
        if col == 0 and d == 0:
            return own[arr].at[rows]
        return held[arr].at[2 * d + col, rows]

    def z_relay(arr, col, h, step, sign):
        if step >= last[arr][sign]:
            return
        here, there = (step * sign) % NZ, ((step + 1) * sign) % NZ
        dst = held[arr].at[2 * there + col, pl.ds(h * HALF, HALF)]
        send((arr, col, h, there), piece(arr, col, h, here), dst, z_dev[sign])

    def x_send(arr, h, d):
        dst = held[arr].at[2 * d + 1, pl.ds(h * HALF, HALF)]
        send((arr, "x", h, d), piece(arr, 0, h, d), dst, x_dev)

    def z_first(arr):
        for h in (0, 1):
            for sign in (1, -1):
                z_relay(arr, 0, h, 0, sign)

    def x_first(arr):
        x_send(arr, 0, 0)
        x_send(arr, 1, 0)

    def x_relay(arr):
        copies[arr, "x", 0, 0].wait_recv()
        for sign in (1, -1):
            z_relay(arr, 1, 0, 0, sign)

    def z_stage(arr, step):
        for col, h in ((0, 0), (0, 1), (1, 0)):
            for sign in (1, -1):
                if step > last[arr][sign]:
                    continue
                d = (step * sign) % NZ
                copies[arr, col, h, d].wait_recv()
                z_relay(arr, col, h, step, sign)
                if (col, h) == (0, 1):
                    x_send(arr, 1, d)

    def x_stage(arr, d):
        copies[arr, "x", 1, d].wait_recv()

    y_last = {0: {1: 4, -1: 3}, 1: {1: 4, -1: 3}, 2: {1: 3, -1: 4}, 3: {1: 3, -1: 4}}

    def bank_at(e, dy):
        return lax.rem(xh + NH - e, NH) * NY + lax.rem(y + NY - dy, NY)

    def y_relay(e, step, sign):
        if step >= y_last[e][sign]:
            return
        here, there = (step * sign) % NY, ((step + 1) * sign) % NY
        at = bank_at(e, here)
        src = items_hbm if (e, here) == (0, 0) else bank.at[at]
        send(("b", e, there), src, bank.at[at], y_dev[sign])

    def y_stage(e, step):
        for sign in (1, -1):
            if step > y_last[e][sign]:
                continue
            copies["b", e, (step * sign) % NY].wait_recv()
            y_relay(e, step, sign)

    def h_relay(e):
        copies["h", e].wait_recv()
        for sign in (1, -1):
            y_relay(e, 0, sign)

    z_first("p")
    x_first("p")
    for sign in (1, -1):
        y_relay(0, 0, sign)
    for e in (1, 3, 2):
        send(("h", e), items_hbm, bank.at[m], h_dev[e])
    send("cq", q_hbm, q_chip.at[1], c_dev)
    send("cp", p_hbm, p_chip.at[1], c_dev)
    z_first("q")
    x_first("q")

    for copy in local:
        copy.wait()
    sub, lane = iota((ROWS, ROWS), 0), iota((ROWS, ROWS), 1)
    upper = (sub <= lane).astype(F32).astype(BF)
    lower = (lane < sub).astype(F32).astype(BF)
    count = counts_v[...].astype(F32)
    count_bf = count.astype(BF)
    ends = nn(count_bf, upper) + jnp.sum(nn(lower, count_bf), axis=1, keepdims=True)
    ends = ends - (m * GROUP).astype(F32)
    starts = ends - count
    inside = (ends > 0.0) & (starts < float(GROUP))
    before = pltpu.roll(count, 1, 1)
    before = jnp.where(lane == 0, pltpu.roll(before, 1, 0), before)
    dd_ref[...] = jnp.where(starts <= 0.0, count, count - before)
    starts = jnp.maximum(starts, 0.0)
    high = jnp.floor(starts * (1.0 / ROWS))
    lo_ref[...] = starts - high * ROWS
    hi_ref[...] = jnp.where(inside, high, 999.0)
    passed = jnp.sum((ends[:, ROWS - 1 :] <= 0.0).astype(F32))
    first = jnp.minimum(passed.astype(jnp.int32), ROWS - WINDOW)
    sub32 = iota((BLOCKS, ROWS), 0).astype(F32)
    subf = sub.astype(F32)

    def scatter(step, total):
        lefts, rights = [], []
        for k in range(2):
            at = pl.ds(first + 2 * step + k, 1)
            same = hi_ref[at, :] == sub32
            mark = jnp.where(same, 1.0, 0.0)
            delta = jnp.where(same, dd_ref[at, :], 0.0)
            lefts.append(jnp.concatenate([mark, delta], axis=0).astype(BF))
            rights.append(jnp.where(lo_ref[at, :] == subf, 1.0, 0.0).astype(BF))
        return total + nt(jnp.concatenate(lefts, axis=1), jnp.concatenate(rights, axis=1))

    marks = lax.fori_loop(0, WINDOW // 2, scatter, jnp.zeros((2 * BLOCKS, ROWS), F32))
    low32 = (iota((BLOCKS, BLOCKS), 1) < iota((BLOCKS, BLOCKS), 0)).astype(F32).astype(BF)

    def running(part):
        part = part.astype(BF)
        return nn(part, upper) + jnp.sum(nn(low32, part), axis=1, keepdims=True)

    reqf[...] = running(marks[:BLOCKS])
    wf[...] = 1.0 / running(marks[BLOCKS:])
    idf[...] = ids_v[...].astype(F32)
    shf[...] = -logq_v[...].astype(F32) * UNIT
    chip_rows = (b, b + 1 - 2 * core)
    for k, at in enumerate(chip_rows):
        rows = pl.ds(k * ROWS, ROWS)
        id_c[rows, :] = as_rows(idf[pl.ds(at, 1), :])
        req_c[rows, :] = as_rows(reqf[pl.ds(at, 1), :])
        sh_c[rows, :] = as_rows(shf[pl.ds(at, 1), :])

    def pair_row(ref, d):
        z_at = lax.rem(z + NZ - d, NZ)
        parts = [ref[pl.ds(x_at * (2 * NZ) + z_at * 2 + core, 1), :] for x_at in (xl, 1 - xl)]
        return jnp.concatenate(parts, axis=1)

    def wide(ref):
        part = ref[...]
        return jnp.concatenate([part, part], axis=1)

    def keep_pair(d):
        keep = (wide(id_c) != pair_row(idf, d)) & (wide(req_c) != pair_row(reqf, d))
        if d == 0:
            keep = keep | (iota((2 * ROWS, 2 * ROWS), 0) == iota((2 * ROWS, 2 * ROWS), 1)) & (
                iota((2 * ROWS, 2 * ROWS), 0) < ROWS
            )
        return keep

    def both(ref):
        return ref[...].reshape(2 * ROWS, DIM)

    def pair(ref, d):
        return ref[2 * d : 2 * d + 2].reshape(2 * ROWS, DIM)

    def row_block(d):
        s = TEMP * nt(both(q_chip), pair(p_all, d)) + pair_row(shf, d)
        s = jnp.where(keep_pair(d), s, NEG)
        s_ref[d] = s
        top = jnp.maximum(s[:, :ROWS], s[:, ROWS:])
        mx_ref[...] = top if d == 0 else jnp.maximum(mx_ref[...], top)

    def col_block(d):
        t = TEMP * nt(both(p_chip), pair(q_all, d)) + wide(sh_c)
        t_ref[d] = jnp.where(keep_pair(d), t, NEG)

    x_relay("p")
    z_stage("p", 1)
    copies["cq"].wait_recv()
    copies["cp"].wait_recv()
    y_stage(0, 1)
    x_stage("p", 0)
    row_block(0)
    x_relay("q")
    z_stage("p", 2)
    h_relay(1)
    h_relay(3)
    x_stage("p", 1)
    row_block(1)
    x_stage("p", 7)
    row_block(7)
    y_stage(0, 2)
    z_stage("p", 3)
    h_relay(2)
    y_stage(1, 1)
    y_stage(3, 1)
    z_stage("q", 1)
    x_stage("p", 2)
    row_block(2)
    x_stage("p", 6)
    row_block(6)
    z_stage("p", 4)
    y_stage(0, 3)
    y_stage(2, 1)
    y_stage(1, 2)
    y_stage(3, 2)
    z_stage("q", 2)
    x_stage("p", 3)
    row_block(3)
    x_stage("p", 5)
    row_block(5)
    y_stage(0, 4)
    y_stage(2, 2)
    y_stage(1, 3)
    y_stage(3, 3)
    x_stage("p", 4)
    row_block(4)

    row_max = jnp.maximum(jnp.max(mx_ref[...], axis=1, keepdims=True), FLOOR)
    lane_sum = jnp.zeros((2 * ROWS, ROWS), F32)
    for d in range(NZ):
        e = jnp.exp(s_ref[d] - row_max)
        lane_sum = lane_sum + e[:, :ROWS] + e[:, ROWS:]
        e_ref[d] = e.astype(BF)
    row_sum = jnp.sum(lane_sum, axis=1, keepdims=True)
    max_a, sum_a = as_row(row_max[:ROWS]), as_row(row_sum[:ROWS])
    max_p, sum_p = as_row(row_max[ROWS:]), as_row(row_sum[ROWS:])
    stat_out[...] = jnp.where(iota((8, ROWS), 0) == 0, max_p, sum_p)
    send("stat", stat_out, stat_in, c_dev)

    z_stage("q", 3)
    y_stage(1, 4)
    y_stage(2, 3)
    y_stage(3, 4)
    y_stage(2, 4)

    q_own = q_chip[0]
    bank_max = None
    for k in range(BANK // ROWS):
        items = bank[4 * k : 4 * k + 4].reshape(ROWS, DIM)
        at = pl.ds(k, 1)
        shift = -blogq_v[at, :].astype(F32) * UNIT
        keep = (bids_v[at, :].astype(F32) != id_c[:ROWS, :]) & (bage_v[at, :] < AGE_LIMIT)
        s = jnp.where(keep, TEMP * nt(q_own, items) + shift, NEG)
        sm_ref[k] = s
        bank_max = s if k == 0 else jnp.maximum(bank_max, s)
    max_m = jnp.maximum(jnp.max(bank_max, axis=1, keepdims=True), FLOOR)
    lane_sum = jnp.zeros((ROWS, ROWS), F32)
    for k in range(BANK // ROWS):
        e = jnp.exp(sm_ref[k] - max_m)
        lane_sum = lane_sum + e
        em_ref[:, k * ROWS : (k + 1) * ROWS] = e.astype(BF)
    max_c, sum_c = as_row(max_m), as_row(jnp.sum(lane_sum, axis=1, keepdims=True))

    copies["stat"].wait_recv()
    max_b, sum_b = stat_in[0:1, :], stat_in[1:2, :]
    top = jnp.maximum(jnp.maximum(max_a, max_b), max_c)
    total = sum_a * jnp.exp(max_a - top) + sum_b * jnp.exp(max_b - top) + sum_c * jnp.exp(max_c - top)
    lse = top + jnp.log(total)
    lse_all[0] = jnp.broadcast_to(lse, (8, ROWS))
    for step in (4, 3, 2, 1, 0):
        for d in sorted({step, (NZ - step) % NZ}):
            for col in (1, 0):
                if (col, d) != (0, 0):
                    device = on_batch(xl if col == 0 else 1 - xl, lax.rem(z + d, NZ), core)
                    send(("lse", col, d), lse_all.at[0], lse_all.at[2 * d + col], device)

    z_stage("q", 4)
    for d in range(NZ):
        part = nn(e_ref[d], pair(p_all, d))
        q_acc[...] = part if d == 0 else q_acc[...] + part
    half_out[...] = q_acc[ROWS:, :]
    send("half", half_out, half_in, c_dev)
    mem_part = nn(em_ref[...], bank[...].reshape(BANK, DIM))

    x_stage("q", 0)
    col_block(0)
    for d in (1, 7, 2, 6, 3, 5, 4):
        x_stage("q", d)
        col_block(d)

    for d in (0, 1, 7, 2, 6, 3, 5, 4):
        for col in (0, 1):
            if (col, d) != (0, 0):
                copies["lse", col, d].wait_recv()
        level = jnp.concatenate([lse_all[2 * d][0:1, :], lse_all[2 * d + 1][0:1, :]], axis=1)
        coef = (jnp.exp(t_ref[d] - level) * pair_row(wf, d)).astype(BF)
        part = nn(coef, pair(q_all, d))
        p_acc[...] = part if d == 0 else p_acc[...] + part
    col_out[...] = p_acc[ROWS:, :]
    send("col", col_out, col_in, c_dev)

    weight = wf[pl.ds(b, 1), :]
    scale = TEMP * weight
    fact_a = as_rows(scale * jnp.exp(max_a - lse))[:, 0:1]
    fact_b = as_rows(scale * jnp.exp(max_b - lse))[:, 0:1]
    fact_c = as_rows(scale * jnp.exp(max_c - lse))[:, 0:1]
    own_term = as_rows(scale)[:, 0:1]
    q_f, p_f = q_chip[0].astype(F32), p_chip[0].astype(F32)
    copies["half"].wait_recv()
    qgrad_out[...] = (
        fact_a * q_acc[:ROWS, :] + fact_b * half_in[...] + fact_c * mem_part - own_term * p_f
    )
    own_logit = TEMP * as_row(jnp.sum(q_f * p_f, axis=1, keepdims=True)) + shf[pl.ds(b, 1), :]
    loss_out[...] = lse - own_logit
    copies["col"].wait_recv()
    pgrad_out[...] = TEMP * (p_acc[:ROWS, :] + col_in[...]) - own_term * q_f

    for copy in copies.values():
        copy.wait_send()


def body(queries, positives, pos_ids, pos_logq, mem_items, mem_ids, mem_logq, mem_age, counts):
    def lines(array):
        return array.reshape(-1, ROWS)

    any_spec = pl.BlockSpec(memory_space=pl.ANY)
    vmem_spec = pl.BlockSpec(memory_space=pltpu.VMEM)
    vmem = pltpu.VMEM
    scratch = [
        vmem((2 * NZ, ROWS, DIM), BF),
        vmem((2 * NZ, ROWS, DIM), BF),
        vmem((2, ROWS, DIM), BF),
        vmem((2, ROWS, DIM), BF),
        vmem((BLOCKS, SLOTS, DIM), BF),
        vmem((NZ, 2 * ROWS, 2 * ROWS), F32),
        vmem((NZ, 2 * ROWS, 2 * ROWS), F32),
        vmem((NZ, 2 * ROWS, 2 * ROWS), BF),
        vmem((2 * ROWS, ROWS), F32),
        vmem((ROWS, ROWS), jnp.int32),
        vmem((BLOCKS, ROWS), jnp.int32),
        vmem((BLOCKS, ROWS), jnp.int32),
        vmem((8, ROWS), jnp.int32),
        vmem((8, ROWS), jnp.int32),
        vmem((8, ROWS), jnp.int32),
        vmem((ROWS, ROWS), F32),
        vmem((ROWS, ROWS), F32),
        vmem((ROWS, ROWS), F32),
        vmem((BLOCKS, ROWS), F32),
        vmem((BLOCKS, ROWS), F32),
        vmem((BLOCKS, ROWS), F32),
        vmem((BLOCKS, ROWS), F32),
        vmem((2 * ROWS, ROWS), F32),
        vmem((2 * ROWS, ROWS), F32),
        vmem((2 * ROWS, ROWS), F32),
        vmem((8, ROWS), F32),
        vmem((8, ROWS), F32),
        vmem((2 * NZ, 8, ROWS), F32),
        vmem((ROWS, DIM), F32),
        vmem((ROWS, DIM), F32),
        vmem((ROWS, DIM), F32),
        vmem((ROWS, DIM), F32),
        vmem((2 * ROWS, DIM), F32),
        vmem((2 * ROWS, DIM), F32),
        vmem((BANK // ROWS, ROWS, ROWS), F32),
        vmem((ROWS, BANK), BF),
        pltpu.SemaphoreType.DMA((SEMS,)),
        pltpu.SemaphoreType.DMA((SEMS,)),
        pltpu.SemaphoreType.DMA((16,)),
    ]
    loss, query_grad, positive_grad = pl.pallas_call(
        kernel,
        out_shape=(
            jax.ShapeDtypeStruct((1, ROWS), F32),
            jax.ShapeDtypeStruct((ROWS, DIM), F32),
            jax.ShapeDtypeStruct((ROWS, DIM), F32),
        ),
        in_specs=[any_spec] * 9,
        out_specs=(vmem_spec, vmem_spec, vmem_spec),
        scratch_shapes=scratch,
        compiler_params=pltpu.CompilerParams(
            collective_id=0, has_side_effects=True, vmem_limit_bytes=40 << 20
        ),
        name="retrieval",
    )(
        queries, positives, mem_items, lines(counts), lines(pos_ids), lines(pos_logq),
        lines(mem_ids), lines(mem_logq), lines(mem_age),
    )
    return loss.reshape(ROWS), query_grad, positive_grad


def solution(mesh):
    in_specs = (
        P(("mem", "batch"), None),
        P(("mem", "batch"), None),
        P(),
        P(),
        P(("batch", "mem"), None),
        P(),
        P(),
        P(),
        P(),
    )
    out_specs = (P(("mem", "batch")), P(("mem", "batch"), None), P(("mem", "batch"), None))
    return jax.shard_map(body, mesh=mesh, in_specs=in_specs, out_specs=out_specs, check_vma=False)
```

```python
import jax
import jax.numpy as jnp
from jax import lax
from jax.experimental import pallas as pl
from jax.experimental.pallas import tpu as pltpu
from jax.sharding import PartitionSpec as P

MESH = pl.DeviceIdType.MESH
AGE_LIMIT = 16
NZ, NY, NH = 8, 8, 4
ROWS, DIM, HALF = 128, 256, 64
BLOCKS = 32
GROUP = ROWS * BLOCKS
SLOTS = 32
BANK = 1024
WINDOW = 34
TEMP = 8.0
UNIT = 1.0 / 1024.0
NEG = -1e30
FLOOR = -1e20
SEMS = 136
BF, F32 = jnp.bfloat16, jnp.float32


def nt(left, right):
    return lax.dot_general(left, right, (((1,), (1,)), ((), ())), preferred_element_type=F32)


def nn(left, right):
    return lax.dot_general(left, right, (((1,), (0,)), ((), ())), preferred_element_type=F32)


def iota(shape, dim):
    return lax.broadcasted_iota(jnp.int32, shape, dim)


def as_rows(row):
    return jnp.broadcast_to(row, (ROWS, ROWS)).T


def as_row(column):
    return jnp.broadcast_to(column, (ROWS, ROWS)).T[0:1, :]


def kernel(
    q_hbm, p_hbm, items_hbm, counts_hbm, ids_hbm, logq_hbm, bids_hbm, blogq_hbm, bage_hbm,
    loss_out, qgrad_out, pgrad_out,
    q_all, p_all, q_chip, p_chip, bank,
    s_ref, t_ref, e_ref, mx_ref,
    counts_v, ids_v, logq_v, bids_v, blogq_v, bage_v,
    hi_ref, lo_ref, dd_ref, idf, reqf, shf, wf, id_c, req_c, sh_c,
    stat_out, stat_in, lse_all, half_out, half_in, col_out, col_in, q_acc, p_acc,
    sm_ref, em_ref,
    send_sems, recv_sems, local_sems, token,
):
    b = lax.axis_index("batch")
    m = lax.axis_index("mem")
    core = lax.rem(b, 2)
    z = lax.rem(lax.div(b, 2), NZ)
    xl = lax.div(b, 2 * NZ)
    y = lax.rem(m, NY)
    xh = lax.div(m, NY)

    def on_batch(x_at, z_at, core_at):
        return {"batch": x_at * (2 * NZ) + z_at * 2 + core_at, "mem": m}

    def on_mem(h_at, y_at):
        return {"batch": b, "mem": h_at * NY + y_at}

    x_dev = on_batch(1 - xl, z, core)
    c_dev = on_batch(xl, z, 1 - core)
    y_next = {1: lax.rem(y + 1, NY), -1: lax.rem(y + NY - 1, NY)}
    y_dev = {s: on_mem(xh, y_next[s]) for s in (1, -1)}
    h_dev = {e: on_mem(lax.rem(xh + e, NH), y) for e in (1, 2, 3)}
    z_up, z_down = lax.rem(z + 1, NZ), lax.rem(z + NZ - 1, NZ)
    up_dev, down_dev = on_batch(xl, z_up, core), on_batch(xl, z_down, core)

    sent = []

    def remote(src, dst, send_at, recv_at, device):
        return pltpu.make_async_remote_copy(
            src_ref=src,
            dst_ref=dst,
            send_sem=send_sems.at[send_at],
            recv_sem=recv_sems.at[recv_at],
            device_id=device,
            device_id_type=MESH,
        )

    def send(src, dst, send_at, recv_at, device):
        copy = remote(src, dst, send_at, recv_at, device)
        copy.start()
        sent.append((None, copy))

    def received(ref, recv_at):
        remote(ref, ref, 0, recv_at, x_dev).wait_recv()

    local = []

    def load(src, dst):
        copy = pltpu.make_async_copy(src, dst, local_sems.at[len(local)])
        copy.start()
        local.append(copy)

    load(counts_hbm, counts_v)
    load(ids_hbm.at[pl.ds(m * BLOCKS, BLOCKS)], ids_v)
    load(logq_hbm.at[pl.ds(m * BLOCKS, BLOCKS)], logq_v)
    load(q_hbm, q_all.at[2 * z])
    load(p_hbm, p_all.at[2 * z])
    load(q_hbm, q_chip.at[0])
    load(p_hbm, p_chip.at[0])
    load(items_hbm, bank.at[m])
    load(bids_hbm.at[pl.ds(b * 8, 8)], bids_v)
    load(blogq_hbm.at[pl.ds(b * 8, 8)], blogq_v)
    load(bage_hbm.at[pl.ds(b * 8, 8)], bage_v)

    barrier = pltpu.get_barrier_semaphore()

    def greet(device):
        pl.semaphore_signal(barrier, inc=1, device_id=device, device_id_type=MESH)

    near = [x_dev, c_dev, y_dev[1], y_dev[-1], h_dev[1], h_dev[2], h_dev[3]]
    for device in near:
        greet(device)
    pl.when(z < NZ - 1)(lambda: greet(up_dev))
    pl.when(z > 0)(lambda: greet(down_dev))
    pl.semaphore_wait(barrier, len(near) + (z < NZ - 1).astype(jnp.int32) + (z > 0).astype(jnp.int32))

    @pl.when(z > 0)
    def _():
        pl.semaphore_wait(token, 1)

    @pl.when(z < NZ - 1)
    def _():
        pl.semaphore_signal(token, inc=1, device_id=up_dev, device_id_type=MESH)

    own = {"q": q_hbm, "p": p_hbm}
    held = {"q": q_all, "p": p_all}
    number = {"p": 0, "q": 1}
    pieces = ((0, 0), (0, 1), (1, 0))
    reach = (5, 5, 5, 4, 3, 2, 2, 2)

    def half(arr, k, col, h):
        return held[arr].at[2 * k + col, pl.ds(h * HALF, HALF)]

    def z_recv(arr, k, piece):
        return number[arr] * 24 + k * 3 + piece

    own_z, own_x, relays, x_relays = {}, {}, {}, {}
    for arr in ("p", "q"):
        n = number[arr]
        for piece, (col, h) in enumerate(pieces):
            here = own[arr].at[pl.ds(h * HALF, HALF)] if col == 0 else half(arr, z, col, h)
            for way, device in ((0, up_dev), (1, down_dev)):
                own_z[arr, piece, way] = remote(
                    here, half(arr, z, col, h), (n * 3 + piece) * 2 + way, z_recv(arr, z, piece), device
                )
            for k in range(NZ):
                step = lax.rem(z - k + NZ, NZ)
                target = jnp.where(step <= reach[k], z_up, z_down)
                relays[arr, k, piece] = remote(
                    half(arr, k, col, h), half(arr, k, col, h), 12 + n * 24 + k * 3 + piece,
                    z_recv(arr, k, piece), on_batch(xl, target, core),
                )
        for h in (0, 1):
            own_x[arr, h] = remote(
                own[arr].at[pl.ds(h * HALF, HALF)], half(arr, z, 1, h),
                76 + n if h == 0 else 60 + n * NZ + z, 64 + n if h == 0 else 48 + n * NZ + z, x_dev,
            )
        for k in range(NZ):
            x_relays[arr, k] = remote(
                half(arr, k, 0, 1), half(arr, k, 1, 1), 60 + n * NZ + k, 48 + n * NZ + k, x_dev
            )

    def begin(copy, when=None):
        if when is None:
            copy.start()
        else:
            pl.when(when)(copy.start)
        sent.append((when, copy))

    def own_first(arr):
        for piece in (0, 1):
            begin(own_z[arr, piece, 0])
            begin(own_z[arr, piece, 1], z > 0)
        for h in (0, 1):
            begin(own_x[arr, h])

    def own_second(arr):
        received(half(arr, z, 1, 0), 64 + number[arr])
        begin(own_z[arr, 2, 0])
        begin(own_z[arr, 2, 1], z > 0)

    def handle(arr, k, when, onward):
        def steps():
            for piece, (col, h) in enumerate(pieces):
                received(half(arr, k, col, h), z_recv(arr, k, piece))
                pl.when(onward)(relays[arr, k, piece].start)
                if piece == 1:
                    x_relays[arr, k].start()

        pl.when(when)(steps)
        for piece in range(3):
            sent.append((when & onward, relays[arr, k, piece]))
        sent.append((when, x_relays[arr, k]))

    def line(arr, k, when=None):
        step = lax.rem(z - k + NZ, NZ)
        onward = ((step > 0) & (step < reach[k])) | (step > reach[k] + 1)
        here = z != k
        if k == 0:
            here = here & (z < NZ - 2)
        if k == 1:
            here = here & (z < NZ - 1)
            onward = onward & (z > 0)
        handle(arr, k, here if when is None else here & when, onward)

    def around(arr):
        for piece in range(3):
            begin(own_z[arr, piece, 1], z == 0)
        for piece in range(3):
            begin(relays[arr, 1, piece], z == 0)
        handle(arr, 0, z >= NZ - 2, z == NZ - 1)
        handle(arr, 1, z == NZ - 1, z < 0)

    def x_stage(arr, k):
        received(half(arr, k, 1, 1), 48 + number[arr] * NZ + k)

    y_last = {0: {1: 4, -1: 3}, 1: {1: 4, -1: 3}, 2: {1: 3, -1: 4}, 3: {1: 3, -1: 4}}

    def bank_at(e, dy):
        return lax.rem(xh + NH - e, NH) * NY + lax.rem(y + NY - dy, NY)

    def y_relay(e, step, sign):
        if step >= y_last[e][sign]:
            return
        here, there = (step * sign) % NY, ((step + 1) * sign) % NY
        at = bank_at(e, here)
        src = items_hbm if (e, here) == (0, 0) else bank.at[at]
        send(src, bank.at[at], 78 + e * NY + there, 66 + e * NY + there, y_dev[sign])

    def y_stage(e, step):
        for sign in (1, -1):
            if step > y_last[e][sign]:
                continue
            d = (step * sign) % NY
            received(bank.at[bank_at(e, d)], 66 + e * NY + d)
            y_relay(e, step, sign)

    def h_relay(e):
        received(bank.at[bank_at(e, 0)], 98 + e)
        for sign in (1, -1):
            y_relay(e, 0, sign)

    own_first("p")
    for sign in (1, -1):
        y_relay(0, 0, sign)
    for e in (1, 3, 2):
        send(items_hbm, bank.at[m], 110 + e, 98 + e, h_dev[e])
    send(q_hbm, q_chip.at[1], 114, 102, c_dev)
    send(p_hbm, p_chip.at[1], 115, 103, c_dev)
    own_first("q")

    for copy in local:
        copy.wait()
    sub, lane = iota((ROWS, ROWS), 0), iota((ROWS, ROWS), 1)
    upper = (sub <= lane).astype(F32).astype(BF)
    lower = (lane < sub).astype(F32).astype(BF)
    count = counts_v[...].astype(F32)
    count_bf = count.astype(BF)
    ends = nn(count_bf, upper) + jnp.sum(nn(lower, count_bf), axis=1, keepdims=True)
    ends = ends - (m * GROUP).astype(F32)
    starts = ends - count
    inside = (ends > 0.0) & (starts < float(GROUP))
    before = pltpu.roll(count, 1, 1)
    before = jnp.where(lane == 0, pltpu.roll(before, 1, 0), before)
    dd_ref[...] = jnp.where(starts <= 0.0, count, count - before)
    starts = jnp.maximum(starts, 0.0)
    high = jnp.floor(starts * (1.0 / ROWS))
    lo_ref[...] = starts - high * ROWS
    hi_ref[...] = jnp.where(inside, high, 999.0)
    passed = jnp.sum((ends[:, ROWS - 1 :] <= 0.0).astype(F32))
    first = jnp.minimum(passed.astype(jnp.int32), ROWS - WINDOW)
    sub32 = iota((BLOCKS, ROWS), 0).astype(F32)
    subf = sub.astype(F32)

    def scatter(step, total):
        lefts, rights = [], []
        for k in range(2):
            at = pl.ds(first + 2 * step + k, 1)
            same = hi_ref[at, :] == sub32
            mark = jnp.where(same, 1.0, 0.0)
            delta = jnp.where(same, dd_ref[at, :], 0.0)
            lefts.append(jnp.concatenate([mark, delta], axis=0).astype(BF))
            rights.append(jnp.where(lo_ref[at, :] == subf, 1.0, 0.0).astype(BF))
        return total + nt(jnp.concatenate(lefts, axis=1), jnp.concatenate(rights, axis=1))

    marks = lax.fori_loop(0, WINDOW // 2, scatter, jnp.zeros((2 * BLOCKS, ROWS), F32))
    low32 = (iota((BLOCKS, BLOCKS), 1) < iota((BLOCKS, BLOCKS), 0)).astype(F32).astype(BF)

    def running(part):
        part = part.astype(BF)
        return nn(part, upper) + jnp.sum(nn(low32, part), axis=1, keepdims=True)

    reqf[...] = running(marks[:BLOCKS])
    wf[...] = 1.0 / running(marks[BLOCKS:])
    idf[...] = ids_v[...].astype(F32)
    shf[...] = -logq_v[...].astype(F32) * UNIT
    chip_rows = (b, b + 1 - 2 * core)
    for k, at in enumerate(chip_rows):
        rows = pl.ds(k * ROWS, ROWS)
        id_c[rows, :] = as_rows(idf[pl.ds(at, 1), :])
        req_c[rows, :] = as_rows(reqf[pl.ds(at, 1), :])
        sh_c[rows, :] = as_rows(shf[pl.ds(at, 1), :])

    def pair_row(ref, k):
        parts = [ref[pl.ds(x_at * (2 * NZ) + k * 2 + core, 1), :] for x_at in (xl, 1 - xl)]
        return jnp.concatenate(parts, axis=1)

    def wide(ref):
        part = ref[...]
        return jnp.concatenate([part, part], axis=1)

    def keep_pair(k):
        keep = (wide(id_c) != pair_row(idf, k)) & (wide(req_c) != pair_row(reqf, k))
        left, right = iota((2 * ROWS, 2 * ROWS), 0), iota((2 * ROWS, 2 * ROWS), 1)
        return keep | ((left == right + (z - k) * GROUP) & (left < ROWS))

    def both(ref):
        return ref[...].reshape(2 * ROWS, DIM)

    def pair(ref, d):
        return ref[2 * d : 2 * d + 2].reshape(2 * ROWS, DIM)

    def row_block(k, first=False):
        x_stage("p", k)
        s = TEMP * nt(both(q_chip), pair(p_all, k)) + pair_row(shf, k)
        s = jnp.where(keep_pair(k), s, NEG)
        s_ref[k] = s
        top = jnp.maximum(s[:, :ROWS], s[:, ROWS:])
        mx_ref[...] = top if first else jnp.maximum(mx_ref[...], top)

    def col_block(k):
        x_stage("q", k)
        t = TEMP * nt(both(p_chip), pair(q_all, k)) + wide(sh_c)
        t_ref[k] = jnp.where(keep_pair(k), t, NEG)

    early = z < 5
    own_second("p")
    line("p", 0)
    line("p", 1)
    y_stage(0, 1)
    line("p", 2)
    h_relay(1)
    h_relay(3)
    own_second("q")
    line("p", 3)
    y_stage(0, 2)
    h_relay(2)
    received(q_chip.at[1], 102)
    received(p_chip.at[1], 103)
    row_block(2, True)
    line("p", 4)
    y_stage(1, 1)
    y_stage(3, 1)
    y_stage(0, 3)
    row_block(3)
    line("p", 5)
    y_stage(2, 1)
    y_stage(1, 2)
    y_stage(3, 2)
    y_stage(0, 4)
    row_block(4)
    for k in range(6):
        line("q", k, early)
    line("p", 6)
    row_block(5)
    line("q", 6)
    y_stage(2, 2)
    y_stage(1, 3)
    y_stage(3, 3)
    line("p", 7)
    row_block(6)
    line("q", 7)
    y_stage(2, 3)
    y_stage(1, 4)
    y_stage(3, 4)
    row_block(7)
    around("p")
    y_stage(2, 4)
    row_block(0)
    row_block(1)

    row_max = jnp.maximum(jnp.max(mx_ref[...], axis=1, keepdims=True), FLOOR)
    lane_sum = jnp.zeros((2 * ROWS, ROWS), F32)
    for d in range(NZ):
        e = jnp.exp(s_ref[d] - row_max)
        lane_sum = lane_sum + e[:, :ROWS] + e[:, ROWS:]
        e_ref[d] = e.astype(BF)
    row_sum = jnp.sum(lane_sum, axis=1, keepdims=True)
    max_a, sum_a = as_row(row_max[:ROWS]), as_row(row_sum[:ROWS])
    max_p, sum_p = as_row(row_max[ROWS:]), as_row(row_sum[ROWS:])
    stat_out[...] = jnp.where(iota((8, ROWS), 0) == 0, max_p, sum_p)
    send(stat_out, stat_in, 116, 104, c_dev)

    q_own = q_chip[0]
    bank_max = None
    for k in range(BANK // ROWS):
        items = bank[4 * k : 4 * k + 4].reshape(ROWS, DIM)
        at = pl.ds(k, 1)
        shift = -blogq_v[at, :].astype(F32) * UNIT
        keep = (bids_v[at, :].astype(F32) != id_c[:ROWS, :]) & (bage_v[at, :] < AGE_LIMIT)
        s = jnp.where(keep, TEMP * nt(q_own, items) + shift, NEG)
        sm_ref[k] = s
        bank_max = s if k == 0 else jnp.maximum(bank_max, s)
    max_m = jnp.maximum(jnp.max(bank_max, axis=1, keepdims=True), FLOOR)
    lane_sum = jnp.zeros((ROWS, ROWS), F32)
    for k in range(BANK // ROWS):
        e = jnp.exp(sm_ref[k] - max_m)
        lane_sum = lane_sum + e
        em_ref[:, k * ROWS : (k + 1) * ROWS] = e.astype(BF)
    max_c, sum_c = as_row(max_m), as_row(jnp.sum(lane_sum, axis=1, keepdims=True))

    received(stat_in, 104)
    max_b, sum_b = stat_in[0:1, :], stat_in[1:2, :]
    top = jnp.maximum(jnp.maximum(max_a, max_b), max_c)
    total = sum_a * jnp.exp(max_a - top) + sum_b * jnp.exp(max_b - top) + sum_c * jnp.exp(max_c - top)
    lse = top + jnp.log(total)
    lse_all[2 * z] = jnp.broadcast_to(lse, (8, ROWS))
    for step in (1, 7, 2, 6, 3, 5, 4, 0):
        for col in (0, 1):
            if (col, step) != (0, 0):
                device = on_batch(xl if col == 0 else 1 - xl, lax.rem(z + step, NZ), core)
                at = 2 * z + col
                send(lse_all.at[2 * z], lse_all.at[at], 119 + 2 * step + col, 107 + at, device)

    for k in range(6):
        line("q", k, z >= 5)
    around("q")
    for d in range(NZ):
        part = nn(e_ref[d], pair(p_all, d))
        q_acc[...] = part if d == 0 else q_acc[...] + part
    half_out[...] = q_acc[ROWS:, :]
    send(half_out, half_in, 117, 105, c_dev)
    mem_part = nn(em_ref[...], bank[...].reshape(BANK, DIM))

    for k in range(NZ):
        col_block(k)

    for k in range(NZ):
        pl.when(z != k)(lambda k=k: received(lse_all.at[2 * k], 107 + 2 * k))
        received(lse_all.at[2 * k + 1], 108 + 2 * k)
        level = jnp.concatenate([lse_all[2 * k][0:1, :], lse_all[2 * k + 1][0:1, :]], axis=1)
        coef = (jnp.exp(t_ref[k] - level) * pair_row(wf, k)).astype(BF)
        part = nn(coef, pair(q_all, k))
        p_acc[...] = part if k == 0 else p_acc[...] + part
    col_out[...] = p_acc[ROWS:, :]
    send(col_out, col_in, 118, 106, c_dev)

    weight = wf[pl.ds(b, 1), :]
    scale = TEMP * weight
    fact_a = as_rows(scale * jnp.exp(max_a - lse))[:, 0:1]
    fact_b = as_rows(scale * jnp.exp(max_b - lse))[:, 0:1]
    fact_c = as_rows(scale * jnp.exp(max_c - lse))[:, 0:1]
    own_term = as_rows(scale)[:, 0:1]
    q_f, p_f = q_chip[0].astype(F32), p_chip[0].astype(F32)
    received(half_in, 105)
    qgrad_out[...] = (
        fact_a * q_acc[:ROWS, :] + fact_b * half_in[...] + fact_c * mem_part - own_term * p_f
    )
    own_logit = TEMP * as_row(jnp.sum(q_f * p_f, axis=1, keepdims=True)) + shf[pl.ds(b, 1), :]
    loss_out[...] = lse - own_logit
    received(col_in, 106)
    pgrad_out[...] = TEMP * (p_acc[:ROWS, :] + col_in[...]) - own_term * q_f

    for when, copy in sent:
        if when is None:
            copy.wait_send()
        else:
            pl.when(when)(copy.wait_send)


def body(queries, positives, pos_ids, pos_logq, mem_items, mem_ids, mem_logq, mem_age, counts):
    def lines(array):
        return array.reshape(-1, ROWS)

    any_spec = pl.BlockSpec(memory_space=pltpu.HBM)
    vmem_spec = pl.BlockSpec(memory_space=pltpu.VMEM)
    vmem = pltpu.VMEM
    scratch = [
        vmem((2 * NZ, ROWS, DIM), BF),
        vmem((2 * NZ, ROWS, DIM), BF),
        vmem((2, ROWS, DIM), BF),
        vmem((2, ROWS, DIM), BF),
        vmem((BLOCKS, SLOTS, DIM), BF),
        vmem((NZ, 2 * ROWS, 2 * ROWS), F32),
        vmem((NZ, 2 * ROWS, 2 * ROWS), F32),
        vmem((NZ, 2 * ROWS, 2 * ROWS), BF),
        vmem((2 * ROWS, ROWS), F32),
        vmem((ROWS, ROWS), jnp.int32),
        vmem((BLOCKS, ROWS), jnp.int32),
        vmem((BLOCKS, ROWS), jnp.int32),
        vmem((8, ROWS), jnp.int32),
        vmem((8, ROWS), jnp.int32),
        vmem((8, ROWS), jnp.int32),
        vmem((ROWS, ROWS), F32),
        vmem((ROWS, ROWS), F32),
        vmem((ROWS, ROWS), F32),
        vmem((BLOCKS, ROWS), F32),
        vmem((BLOCKS, ROWS), F32),
        vmem((BLOCKS, ROWS), F32),
        vmem((BLOCKS, ROWS), F32),
        vmem((2 * ROWS, ROWS), F32),
        vmem((2 * ROWS, ROWS), F32),
        vmem((2 * ROWS, ROWS), F32),
        vmem((8, ROWS), F32),
        vmem((8, ROWS), F32),
        vmem((2 * NZ, 8, ROWS), F32),
        vmem((ROWS, DIM), F32),
        vmem((ROWS, DIM), F32),
        vmem((ROWS, DIM), F32),
        vmem((ROWS, DIM), F32),
        vmem((2 * ROWS, DIM), F32),
        vmem((2 * ROWS, DIM), F32),
        vmem((BANK // ROWS, ROWS, ROWS), F32),
        vmem((ROWS, BANK), BF),
        pltpu.SemaphoreType.DMA((SEMS,)),
        pltpu.SemaphoreType.DMA((SEMS,)),
        pltpu.SemaphoreType.DMA((16,)),
        pltpu.SemaphoreType.REGULAR,
    ]
    loss, query_grad, positive_grad = pl.pallas_call(
        kernel,
        out_shape=(
            jax.ShapeDtypeStruct((1, ROWS), F32),
            jax.ShapeDtypeStruct((ROWS, DIM), F32),
            jax.ShapeDtypeStruct((ROWS, DIM), F32),
        ),
        in_specs=[any_spec] * 9,
        out_specs=(vmem_spec, vmem_spec, vmem_spec),
        scratch_shapes=scratch,
        compiler_params=pltpu.CompilerParams(
            collective_id=0, has_side_effects=True, vmem_limit_bytes=67043328
        ),
        name="retrieval",
    )(
        queries, positives, mem_items, lines(counts), lines(pos_ids), lines(pos_logq),
        lines(mem_ids), lines(mem_logq), lines(mem_age),
    )
    return loss.reshape(ROWS), query_grad, positive_grad


def solution(mesh):
    in_specs = (
        P(("mem", "batch"), None),
        P(("mem", "batch"), None),
        P(),
        P(),
        P(("batch", "mem"), None),
        P(),
        P(),
        P(),
        P(),
    )
    out_specs = (P(("mem", "batch")), P(("mem", "batch"), None), P(("mem", "batch"), None))
    return jax.shard_map(body, mesh=mesh, in_specs=in_specs, out_specs=out_specs, check_vma=False)
```

```python
import jax
import jax.numpy as jnp
from jax import lax
from jax.experimental import pallas as pl
from jax.experimental.pallas import tpu as pltpu
from jax.sharding import PartitionSpec as P

MESH = pl.DeviceIdType.MESH
AGE_LIMIT = 16
NZ, NY, NH = 8, 8, 4
ROWS, DIM, CUT = 128, 256, 32
BLOCKS = 32
GROUP = ROWS * BLOCKS
SLOTS = 32
BANK = 1024
WINDOW = 34
TEMP = 8.0
UNIT = 1.0 / 1024.0
NEG = -1e30
FLOOR = -1e20
SEMS = 192
BF, F32 = jnp.bfloat16, jnp.float32


def nt(left, right):
    return lax.dot_general(left, right, (((1,), (1,)), ((), ())), preferred_element_type=F32)


def nn(left, right):
    return lax.dot_general(left, right, (((1,), (0,)), ((), ())), preferred_element_type=F32)


def iota(shape, dim):
    return lax.broadcasted_iota(jnp.int32, shape, dim)


def as_rows(row):
    return jnp.broadcast_to(row, (ROWS, ROWS)).T


def as_row(column):
    return jnp.broadcast_to(column, (ROWS, ROWS)).T[0:1, :]


def kernel(
    q_hbm, p_hbm, items_hbm, counts_hbm, ids_hbm, logq_hbm, bids_hbm, blogq_hbm, bage_hbm,
    loss_out, qgrad_out, pgrad_out,
    q_all, p_all, q_chip, p_chip, bank,
    s_ref, t_ref, e_ref, mx_ref,
    counts_v, ids_v, logq_v, bids_v, blogq_v, bage_v,
    hi_ref, lo_ref, dd_ref, idf, reqf, shf, wf, id_c, req_c, sh_c,
    stat_out, stat_in, lse_all, half_out, half_in, col_out, col_in, q_acc, p_acc,
    sm_ref, em_ref,
    send_sems, recv_sems, local_sems,
):
    b = lax.axis_index("batch")
    m = lax.axis_index("mem")
    core = lax.rem(b, 2)
    z = lax.rem(lax.div(b, 2), NZ)
    xl = lax.div(b, 2 * NZ)
    y = lax.rem(m, NY)
    xh = lax.div(m, NY)

    def on_batch(x_at, z_at, core_at):
        return {"batch": x_at * (2 * NZ) + z_at * 2 + core_at, "mem": m}

    def on_mem(h_at, y_at):
        return {"batch": b, "mem": h_at * NY + y_at}

    def z_dev(hop):
        return on_batch(xl, lax.rem(z + hop + NZ, NZ), core)

    def y_dev(hop):
        return on_mem(xh, lax.rem(y + hop + NY, NY))

    x_dev = on_batch(1 - xl, z, core)
    c_dev = on_batch(xl, z, 1 - core)
    h_dev = {e: on_mem(lax.rem(xh + e, NH), y) for e in (1, 2, 3)}

    copies = {}

    def send(key, src, dst, device):
        k = len(copies)
        copy = pltpu.make_async_remote_copy(
            src_ref=src,
            dst_ref=dst,
            send_sem=send_sems.at[k],
            recv_sem=recv_sems.at[k],
            device_id=device,
            device_id_type=MESH,
        )
        copy.start()
        copies[key] = copy

    local = []

    def load(src, dst):
        copy = pltpu.make_async_copy(src, dst, local_sems.at[len(local)])
        copy.start()
        local.append(copy)

    load(counts_hbm, counts_v)
    load(ids_hbm.at[pl.ds(m * BLOCKS, BLOCKS)], ids_v)
    load(logq_hbm.at[pl.ds(m * BLOCKS, BLOCKS)], logq_v)
    load(q_hbm, q_all.at[0])
    load(p_hbm, p_all.at[0])
    load(q_hbm, q_chip.at[0])
    load(p_hbm, p_chip.at[0])
    load(items_hbm, bank.at[m])
    load(bids_hbm.at[pl.ds(b * 8, 8)], bids_v)
    load(blogq_hbm.at[pl.ds(b * 8, 8)], blogq_v)
    load(bage_hbm.at[pl.ds(b * 8, 8)], bage_v)

    barrier = pltpu.get_barrier_semaphore()
    near = [place(hop) for place in (z_dev, y_dev) for hop in (1, -1, 2, -2)]
    near += [x_dev, c_dev, h_dev[1], h_dev[2], h_dev[3]]
    for device in near:
        pl.semaphore_signal(barrier, inc=1, device_id=device, device_id_type=MESH)
    pl.semaphore_wait(barrier, len(near))

    own = {"q": q_hbm, "p": p_hbm}
    held = {"q": q_all, "p": p_all}
    onward = {"p": ((2, 1), (2, 2), (6, -1)), "q": ((2, 1), (6, -1), (6, -2))}

    def got(*key):
        copies[key].wait_recv()

    def piece(arr, col, d):
        if col == 0 and d == 0:
            return own[arr]
        return held[arr].at[2 * d] if col == 0 else held[arr].at[2 * d + 1, pl.ds(0, CUT)]

    def z_send(arr, col, d, hop):
        there = (d + hop) % NZ
        block = held[arr].at[2 * there + col]
        dst = block if col == 0 else held[arr].at[2 * there + 1, pl.ds(0, CUT)]
        send((arr, col, there), piece(arr, col, d), dst, z_dev(hop))

    def z_first(arr, col, hops):
        for hop in hops:
            z_send(arr, col, 0, hop)

    def z_relay(arr, col):
        for d in (2, 6):
            got(arr, col, d)
            for start, hop in onward[arr]:
                if start == d:
                    z_send(arr, col, d, hop)

    def x_first(arr):
        src, dst = own[arr].at[pl.ds(0, CUT)], held[arr].at[1, pl.ds(0, CUT)]
        send((arr, "first"), src, dst, x_dev)

    def x_send(arr, d):
        rest = pl.ds(CUT, ROWS - CUT)
        src = own[arr].at[rest] if d == 0 else held[arr].at[2 * d, rest]
        send((arr, "x", d), src, held[arr].at[2 * d + 1, rest], x_dev)

    def x_pass(arr, *blocks):
        for d in blocks:
            if d not in (2, 6):
                got(arr, 0, d)
            x_send(arr, d)

    def second(arr):
        got(arr, "first")
        z_first(arr, 1, (1, -1, 2, -2))

    def have(arr, d):
        got(arr, "x", d)
        if d not in (0, 2, 6):
            got(arr, 1, d)

    def bank_at(e, dy):
        return lax.rem(xh + NH - e, NH) * NY + lax.rem(y + NY - dy, NY)

    def y_send(e, d, hop):
        at = bank_at(e, d)
        src = items_hbm if (e, d) == (0, 0) else bank.at[at]
        send(("b", e, (d + hop) % NY), src, bank.at[at], y_dev(hop))

    def y_first(e):
        if e:
            got("h", e)
        for hop in (1, -1, 2, -2):
            y_send(e, 0, hop)

    def y_relay(e):
        for d, hop in ((2, 1), (2, 2), (6, -1)) if e in (0, 1) else ((2, 1), (6, -1), (6, -2)):
            if (d, hop) != (2, 2) and (d, hop) != (6, -2):
                got("b", e, d)
            y_send(e, d, hop)

    z_first("p", 0, (2, -2, 1, -1))
    x_first("p")
    for e in (1, 3, 2):
        send(("h", e), items_hbm, bank.at[m], h_dev[e])
    y_first(0)
    x_send("p", 0)
    send(("cq",), q_hbm, q_chip.at[1], c_dev)
    send(("cp",), p_hbm, p_chip.at[1], c_dev)
    z_first("q", 0, (1, -1))

    for copy in local:
        copy.wait()
    sub, lane = iota((ROWS, ROWS), 0), iota((ROWS, ROWS), 1)
    upper = (sub <= lane).astype(F32).astype(BF)
    lower = (lane < sub).astype(F32).astype(BF)
    count = counts_v[...].astype(F32)
    count_bf = count.astype(BF)
    ends = nn(count_bf, upper) + jnp.sum(nn(lower, count_bf), axis=1, keepdims=True)
    ends = ends - (m * GROUP).astype(F32)
    starts = ends - count
    inside = (ends > 0.0) & (starts < float(GROUP))
    before = pltpu.roll(count, 1, 1)
    before = jnp.where(lane == 0, pltpu.roll(before, 1, 0), before)
    dd_ref[...] = jnp.where(starts <= 0.0, count, count - before)
    starts = jnp.maximum(starts, 0.0)
    high = jnp.floor(starts * (1.0 / ROWS))
    lo_ref[...] = starts - high * ROWS
    hi_ref[...] = jnp.where(inside, high, 999.0)
    passed = jnp.sum((ends[:, ROWS - 1 :] <= 0.0).astype(F32))
    first = jnp.minimum(passed.astype(jnp.int32), ROWS - WINDOW)
    sub32 = iota((BLOCKS, ROWS), 0).astype(F32)
    subf = sub.astype(F32)

    def scatter(step, total):
        lefts, rights = [], []
        for k in range(2):
            at = pl.ds(first + 2 * step + k, 1)
            same = hi_ref[at, :] == sub32
            mark = jnp.where(same, 1.0, 0.0)
            delta = jnp.where(same, dd_ref[at, :], 0.0)
            lefts.append(jnp.concatenate([mark, delta], axis=0).astype(BF))
            rights.append(jnp.where(lo_ref[at, :] == subf, 1.0, 0.0).astype(BF))
        return total + nt(jnp.concatenate(lefts, axis=1), jnp.concatenate(rights, axis=1))

    marks = lax.fori_loop(0, WINDOW // 2, scatter, jnp.zeros((2 * BLOCKS, ROWS), F32))
    low32 = (iota((BLOCKS, BLOCKS), 1) < iota((BLOCKS, BLOCKS), 0)).astype(F32).astype(BF)

    def running(part):
        part = part.astype(BF)
        return nn(part, upper) + jnp.sum(nn(low32, part), axis=1, keepdims=True)

    reqf[...] = running(marks[:BLOCKS])
    wf[...] = 1.0 / running(marks[BLOCKS:])
    idf[...] = ids_v[...].astype(F32)
    shf[...] = -logq_v[...].astype(F32) * UNIT
    chip_rows = (b, b + 1 - 2 * core)
    for k, at in enumerate(chip_rows):
        rows = pl.ds(k * ROWS, ROWS)
        id_c[rows, :] = as_rows(idf[pl.ds(at, 1), :])
        req_c[rows, :] = as_rows(reqf[pl.ds(at, 1), :])
        sh_c[rows, :] = as_rows(shf[pl.ds(at, 1), :])

    def pair_row(ref, d):
        z_at = lax.rem(z + NZ - d, NZ)
        parts = [ref[pl.ds(x_at * (2 * NZ) + z_at * 2 + core, 1), :] for x_at in (xl, 1 - xl)]
        return jnp.concatenate(parts, axis=1)

    def wide(ref):
        part = ref[...]
        return jnp.concatenate([part, part], axis=1)

    def keep_pair(d):
        keep = (wide(id_c) != pair_row(idf, d)) & (wide(req_c) != pair_row(reqf, d))
        if d == 0:
            keep = keep | (iota((2 * ROWS, 2 * ROWS), 0) == iota((2 * ROWS, 2 * ROWS), 1)) & (
                iota((2 * ROWS, 2 * ROWS), 0) < ROWS
            )
        return keep

    def both(ref):
        return ref[...].reshape(2 * ROWS, DIM)

    def pair(ref, d):
        return ref[2 * d : 2 * d + 2].reshape(2 * ROWS, DIM)

    def row_block(d):
        have("p", d)
        s = TEMP * nt(both(q_chip), pair(p_all, d)) + pair_row(shf, d)
        s = jnp.where(keep_pair(d), s, NEG)
        s_ref[d] = s
        top = jnp.maximum(s[:, :ROWS], s[:, ROWS:])
        mx_ref[...] = top if d == 0 else jnp.maximum(mx_ref[...], top)

    def col_block(d):
        have("q", d)
        t = TEMP * nt(both(p_chip), pair(q_all, d)) + wide(sh_c)
        t_ref[d] = jnp.where(keep_pair(d), t, NEG)

    second("p")
    x_pass("p", 1, 7)
    y_first(1)
    y_first(3)
    z_relay("p", 0)
    y_relay(0)
    x_pass("p", 2, 6)
    y_first(2)
    z_relay("p", 1)
    z_first("q", 0, (2, -2))
    x_first("q")
    x_send("q", 0)
    got("cq")
    got("cp")
    row_block(0)
    row_block(1)
    row_block(7)
    y_relay(1)
    y_relay(3)
    x_pass("p", 3, 5)
    second("q")
    x_pass("p", 4)
    row_block(2)
    row_block(6)
    y_relay(2)
    x_pass("q", 1, 7)
    z_relay("q", 0)
    x_pass("q", 2, 6)
    row_block(3)
    row_block(5)
    z_relay("q", 1)
    row_block(4)

    row_max = jnp.maximum(jnp.max(mx_ref[...], axis=1, keepdims=True), FLOOR)
    lane_sum = jnp.zeros((2 * ROWS, ROWS), F32)
    for d in range(NZ):
        e = jnp.exp(s_ref[d] - row_max)
        lane_sum = lane_sum + e[:, :ROWS] + e[:, ROWS:]
        e_ref[d] = e.astype(BF)
    row_sum = jnp.sum(lane_sum, axis=1, keepdims=True)
    max_a, sum_a = as_row(row_max[:ROWS]), as_row(row_sum[:ROWS])
    max_p, sum_p = as_row(row_max[ROWS:]), as_row(row_sum[ROWS:])
    stat_out[...] = jnp.where(iota((8, ROWS), 0) == 0, max_p, sum_p)
    send(("stat",), stat_out, stat_in, c_dev)

    x_pass("q", 3, 5, 4)
    for e in range(NH):
        for d in (1, 7, 3, 5, 4):
            got("b", e, d)

    q_own = q_chip[0]
    bank_max = None
    for k in range(BANK // ROWS):
        items = bank[4 * k : 4 * k + 4].reshape(ROWS, DIM)
        at = pl.ds(k, 1)
        shift = -blogq_v[at, :].astype(F32) * UNIT
        keep = (bids_v[at, :].astype(F32) != id_c[:ROWS, :]) & (bage_v[at, :] < AGE_LIMIT)
        s = jnp.where(keep, TEMP * nt(q_own, items) + shift, NEG)
        sm_ref[k] = s
        bank_max = s if k == 0 else jnp.maximum(bank_max, s)
    max_m = jnp.maximum(jnp.max(bank_max, axis=1, keepdims=True), FLOOR)
    lane_sum = jnp.zeros((ROWS, ROWS), F32)
    for k in range(BANK // ROWS):
        e = jnp.exp(sm_ref[k] - max_m)
        lane_sum = lane_sum + e
        em_ref[:, k * ROWS : (k + 1) * ROWS] = e.astype(BF)
    max_c, sum_c = as_row(max_m), as_row(jnp.sum(lane_sum, axis=1, keepdims=True))

    got("stat")
    max_b, sum_b = stat_in[0:1, :], stat_in[1:2, :]
    top = jnp.maximum(jnp.maximum(max_a, max_b), max_c)
    total = sum_a * jnp.exp(max_a - top) + sum_b * jnp.exp(max_b - top) + sum_c * jnp.exp(max_c - top)
    lse = top + jnp.log(total)
    lse_all[0] = jnp.broadcast_to(lse, (8, ROWS))
    for d in (4, 3, 5, 2, 6, 1, 7, 0):
        for col in (1, 0):
            if (col, d) != (0, 0):
                device = on_batch(xl if col == 0 else 1 - xl, lax.rem(z + d, NZ), core)
                send(("lse", col, d), lse_all.at[0], lse_all.at[2 * d + col], device)

    for d in range(NZ):
        part = nn(e_ref[d], pair(p_all, d))
        q_acc[...] = part if d == 0 else q_acc[...] + part
    half_out[...] = q_acc[ROWS:, :]
    send(("half",), half_out, half_in, c_dev)
    mem_part = nn(em_ref[...], bank[...].reshape(BANK, DIM))

    for d in (0, 1, 7, 2, 6, 3, 5, 4):
        col_block(d)

    for d in (0, 1, 7, 2, 6, 3, 5, 4):
        for col in (0, 1):
            if (col, d) != (0, 0):
                got("lse", col, d)
        level = jnp.concatenate([lse_all[2 * d][0:1, :], lse_all[2 * d + 1][0:1, :]], axis=1)
        coef = (jnp.exp(t_ref[d] - level) * pair_row(wf, d)).astype(BF)
        part = nn(coef, pair(q_all, d))
        p_acc[...] = part if d == 0 else p_acc[...] + part
    col_out[...] = p_acc[ROWS:, :]
    send(("col",), col_out, col_in, c_dev)

    weight = wf[pl.ds(b, 1), :]
    scale = TEMP * weight
    fact_a = as_rows(scale * jnp.exp(max_a - lse))[:, 0:1]
    fact_b = as_rows(scale * jnp.exp(max_b - lse))[:, 0:1]
    fact_c = as_rows(scale * jnp.exp(max_c - lse))[:, 0:1]
    own_term = as_rows(scale)[:, 0:1]
    q_f, p_f = q_chip[0].astype(F32), p_chip[0].astype(F32)
    got("half")
    qgrad_out[...] = (
        fact_a * q_acc[:ROWS, :] + fact_b * half_in[...] + fact_c * mem_part - own_term * p_f
    )
    own_logit = TEMP * as_row(jnp.sum(q_f * p_f, axis=1, keepdims=True)) + shf[pl.ds(b, 1), :]
    loss_out[...] = lse - own_logit
    got("col")
    pgrad_out[...] = TEMP * (p_acc[:ROWS, :] + col_in[...]) - own_term * q_f

    for copy in copies.values():
        copy.wait_send()


def body(queries, positives, pos_ids, pos_logq, mem_items, mem_ids, mem_logq, mem_age, counts):
    def lines(array):
        return array.reshape(-1, ROWS)

    any_spec = pl.BlockSpec(memory_space=pltpu.HBM)
    vmem_spec = pl.BlockSpec(memory_space=pltpu.VMEM)
    vmem = pltpu.VMEM
    scratch = [
        vmem((2 * NZ, ROWS, DIM), BF),
        vmem((2 * NZ, ROWS, DIM), BF),
        vmem((2, ROWS, DIM), BF),
        vmem((2, ROWS, DIM), BF),
        vmem((BLOCKS, SLOTS, DIM), BF),
        vmem((NZ, 2 * ROWS, 2 * ROWS), F32),
        vmem((NZ, 2 * ROWS, 2 * ROWS), F32),
        vmem((NZ, 2 * ROWS, 2 * ROWS), BF),
        vmem((2 * ROWS, ROWS), F32),
        vmem((ROWS, ROWS), jnp.int32),
        vmem((BLOCKS, ROWS), jnp.int32),
        vmem((BLOCKS, ROWS), jnp.int32),
        vmem((8, ROWS), jnp.int32),
        vmem((8, ROWS), jnp.int32),
        vmem((8, ROWS), jnp.int32),
        vmem((ROWS, ROWS), F32),
        vmem((ROWS, ROWS), F32),
        vmem((ROWS, ROWS), F32),
        vmem((BLOCKS, ROWS), F32),
        vmem((BLOCKS, ROWS), F32),
        vmem((BLOCKS, ROWS), F32),
        vmem((BLOCKS, ROWS), F32),
        vmem((2 * ROWS, ROWS), F32),
        vmem((2 * ROWS, ROWS), F32),
        vmem((2 * ROWS, ROWS), F32),
        vmem((8, ROWS), F32),
        vmem((8, ROWS), F32),
        vmem((2 * NZ, 8, ROWS), F32),
        vmem((ROWS, DIM), F32),
        vmem((ROWS, DIM), F32),
        vmem((ROWS, DIM), F32),
        vmem((ROWS, DIM), F32),
        vmem((2 * ROWS, DIM), F32),
        vmem((2 * ROWS, DIM), F32),
        vmem((BANK // ROWS, ROWS, ROWS), F32),
        vmem((ROWS, BANK), BF),
        pltpu.SemaphoreType.DMA((SEMS,)),
        pltpu.SemaphoreType.DMA((SEMS,)),
        pltpu.SemaphoreType.DMA((16,)),
    ]
    loss, query_grad, positive_grad = pl.pallas_call(
        kernel,
        out_shape=(
            jax.ShapeDtypeStruct((1, ROWS), F32),
            jax.ShapeDtypeStruct((ROWS, DIM), F32),
            jax.ShapeDtypeStruct((ROWS, DIM), F32),
        ),
        in_specs=[any_spec] * 9,
        out_specs=(vmem_spec, vmem_spec, vmem_spec),
        scratch_shapes=scratch,
        compiler_params=pltpu.CompilerParams(
            collective_id=0, has_side_effects=True, vmem_limit_bytes=67043328
        ),
        name="retrieval",
    )(
        queries, positives, mem_items, lines(counts), lines(pos_ids), lines(pos_logq),
        lines(mem_ids), lines(mem_logq), lines(mem_age),
    )
    return loss.reshape(ROWS), query_grad, positive_grad


def solution(mesh):
    in_specs = (
        P(("mem", "batch"), None),
        P(("mem", "batch"), None),
        P(),
        P(),
        P(("batch", "mem"), None),
        P(),
        P(),
        P(),
        P(),
    )
    out_specs = (P(("mem", "batch")), P(("mem", "batch"), None), P(("mem", "batch"), None))
    return jax.shard_map(body, mesh=mesh, in_specs=in_specs, out_specs=out_specs, check_vma=False)
```

```python
import jax
import jax.numpy as jnp
from jax import lax
from jax.experimental import pallas as pl
from jax.experimental.pallas import tpu as pltpu
from jax.sharding import PartitionSpec as P

MESH = pl.DeviceIdType.MESH
AGE_LIMIT = 16
NZ, NY, NH = 8, 8, 4
ROWS, DIM, CUT = 128, 256, 32
BLOCKS = 32
GROUP = ROWS * BLOCKS
SLOTS = 32
BANK = 1024
WINDOW = 34
TEMP = 8.0
UNIT = 1.0 / 1024.0
NEG = -1e30
FLOOR = -1e20
SENDS, ARRIVALS, LOADS = 8, 40, 5
BF, F32 = jnp.bfloat16, jnp.float32


def nt(left, right):
    return lax.dot_general(left, right, (((1,), (1,)), ((), ())), preferred_element_type=F32)


def nn(left, right):
    return lax.dot_general(left, right, (((1,), (0,)), ((), ())), preferred_element_type=F32)


def iota(shape, dim):
    return lax.broadcasted_iota(jnp.int32, shape, dim)


def as_rows(row):
    return jnp.broadcast_to(row, (ROWS, ROWS)).T


def as_row(column):
    return jnp.broadcast_to(column, (ROWS, ROWS)).T[0:1, :]


def kernel(
    q_hbm, p_hbm, items_hbm, counts_hbm, ids_hbm, logq_hbm, bids_hbm, blogq_hbm, bage_hbm,
    loss_out, qgrad_out, pgrad_out,
    q_all, p_all, q_chip, p_chip, bank,
    s_ref, t_ref, e_ref, mx_ref,
    counts_v, lines_v, bank_v,
    hi_ref, lo_ref, dd_ref, idf, reqf, shf, wf, id_c, req_c, sh_c,
    stat_out, stat_in, lse_all, half_out, half_in, col_out, col_in, q_acc, p_acc,
    sm_ref, em_ref,
    send_sems, recv_sems, local_sems,
):
    b = lax.axis_index("batch")
    m = lax.axis_index("mem")
    core = lax.rem(b, 2)
    z = lax.rem(lax.div(b, 2), NZ)
    xl = lax.div(b, 2 * NZ)
    y = lax.rem(m, NY)
    xh = lax.div(m, NY)

    def on_batch(x_at, z_at, core_at):
        return {"batch": x_at * (2 * NZ) + z_at * 2 + core_at, "mem": m}

    def on_mem(h_at, y_at):
        return {"batch": b, "mem": h_at * NY + y_at}

    def z_dev(hop):
        return on_batch(xl, lax.rem(z + hop + NZ, NZ), core)

    def y_dev(hop):
        return on_mem(xh, lax.rem(y + hop + NY, NY))

    x_dev = on_batch(1 - xl, z, core)
    c_dev = on_batch(xl, z, 1 - core)
    h_dev = {e: on_mem(lax.rem(xh + e, NH), y) for e in (1, 3)}

    send_at, arrive_at = {}, {}

    def send(out, into, src, dst, device):
        pltpu.make_async_remote_copy(
            src_ref=src,
            dst_ref=dst,
            send_sem=send_sems.at[send_at.setdefault(out, len(send_at))],
            recv_sem=recv_sems.at[arrive_at.setdefault(into, len(arrive_at))],
            device_id=device,
            device_id_type=MESH,
        ).start()

    def waiting(sem, ref):
        pltpu.make_async_copy(ref, ref, sem).wait()

    def sent(out, ref):
        waiting(send_sems.at[send_at[out]], ref)

    def got(into, ref):
        waiting(recv_sems.at[arrive_at[into]], ref)

    def load(kind, src, dst):
        pltpu.make_async_copy(src, dst, local_sems.at[kind]).start()

    load(0, counts_hbm, counts_v)
    load(1, ids_hbm.at[pl.ds(m * BLOCKS, BLOCKS)], lines_v.at[0])
    load(1, logq_hbm.at[pl.ds(m * BLOCKS, BLOCKS)], lines_v.at[1])
    load(2, bids_hbm.at[pl.ds(b * 8, 8)], bank_v.at[0])
    load(2, blogq_hbm.at[pl.ds(b * 8, 8)], bank_v.at[1])
    load(2, bage_hbm.at[pl.ds(b * 8, 8)], bank_v.at[2])
    load(3, q_hbm, q_all.at[0])
    load(3, p_hbm, p_all.at[0])
    load(3, q_hbm, q_chip.at[0])
    load(3, p_hbm, p_chip.at[0])
    load(4, items_hbm, bank.at[m])

    barrier = pltpu.get_barrier_semaphore()
    near = [place(hop) for place in (z_dev, y_dev) for hop in (1, -1, 2, -2)]
    near += [x_dev, c_dev, h_dev[1], h_dev[3]]
    for device in near:
        pl.semaphore_signal(barrier, inc=1, device_id=device, device_id_type=MESH)
    pl.semaphore_wait(barrier, len(near))

    own = {"q": q_hbm, "p": p_hbm}
    held = {"q": q_all, "p": p_all}
    onward = {"p": ((2, 1), (2, 2), (6, -1)), "q": ((2, 1), (6, -1), (6, -2))}

    def blocks(arr, n):
        return held[arr].at[pl.ds(0, n)]

    def piece(arr, col, d):
        if col == 0 and d == 0:
            return own[arr]
        return held[arr].at[2 * d] if col == 0 else held[arr].at[2 * d + 1, pl.ds(0, CUT)]

    near_far = {1: 1, 7: 1, 2: 2, 6: 2, 3: 3, 5: 3, 4: 3}
    final = {1: "near", 7: "near", 3: "far", 5: "far", 4: "last"}

    def z_send(arr, col, d, hop):
        there = (d + hop) % NZ
        block = held[arr].at[2 * there + col]
        dst = block if col == 0 else held[arr].at[2 * there + 1, pl.ds(0, CUT)]
        into = near_far[there] if col == 0 else final.get(there, "cut")
        send(arr, (arr, into), piece(arr, col, d), dst, z_dev(hop))

    def z_first(arr, col, hops):
        for hop in hops:
            z_send(arr, col, 0, hop)

    def z_relay(arr, col):
        got((arr, 2), blocks(arr, 2)) if col == 0 else got((arr, "cut"), held[arr].at[1, pl.ds(0, 2 * CUT)])
        for d, hop in onward[arr]:
            z_send(arr, col, d, hop)

    def x_first(arr):
        src, dst = own[arr].at[pl.ds(0, CUT)], held[arr].at[1, pl.ds(0, CUT)]
        send(arr, (arr, "first"), src, dst, x_dev)

    def x_send(arr, d):
        rest = pl.ds(CUT, ROWS - CUT)
        src = own[arr].at[rest] if d == 0 else held[arr].at[2 * d, rest]
        into = final.get(d, "x0" if d == 0 else "x2")
        send(arr, (arr, into), src, held[arr].at[2 * d + 1, rest], x_dev)

    def x_pass(arr, *group):
        if group[0] == 1:
            got((arr, 1), blocks(arr, 2))
        if group[0] == 3:
            got((arr, 3), blocks(arr, 3))
        for d in group:
            x_send(arr, d)

    def second(arr):
        got((arr, "first"), held[arr].at[1, pl.ds(0, CUT)])
        z_first(arr, 1, (1, -1, 2, -2))

    def have(arr, d):
        rest = ROWS - CUT
        if d == 0:
            got((arr, "x0"), held[arr].at[1, pl.ds(0, rest)])
        if d == 2:
            got((arr, "x2"), held[arr].at[pl.ds(0, 2), pl.ds(0, rest)])
        if d in (1, 3):
            got((arr, final[d]), blocks(arr, 2))
        if d == 4:
            got((arr, final[d]), blocks(arr, 1))

    def bank_at(e, dy):
        return lax.rem(xh + NH - e, NH) * NY + lax.rem(y + NY - dy, NY)

    def y_send(e, d, hop):
        at, there = bank_at(e, d), (d + hop) % NY
        src = items_hbm if (e, d) == (0, 0) else bank.at[at]
        into = ("bank", e) if there in (2, 6) else "bank"
        send("bank", into, src, bank.at[at], y_dev(hop))

    def y_first(e):
        if e:
            got(("h", e), bank.at[0])
        if e == 1:
            send("bank", ("h", 2), bank.at[bank_at(1, 0)], bank.at[bank_at(1, 0)], h_dev[1])
        for hop in (1, -1, 2, -2):
            y_send(e, 0, hop)

    def y_relay(e):
        got(("bank", e), bank.at[pl.ds(0, 2)])
        for d, hop in ((2, 1), (2, 2), (6, -1)) if e in (0, 1) else ((2, 1), (6, -1), (6, -2)):
            y_send(e, d, hop)

    z_first("p", 0, (2, -2, 1, -1))
    x_first("p")
    for e in (1, 3):
        send("bank", ("h", e), items_hbm, bank.at[m], h_dev[e])
    y_first(0)
    x_send("p", 0)
    send("chip", "chip", q_hbm, q_chip.at[1], c_dev)
    send("chip", "chip", p_hbm, p_chip.at[1], c_dev)
    z_first("q", 0, (1, -1))

    waiting(local_sems.at[0], counts_v)
    waiting(local_sems.at[1], lines_v)
    waiting(local_sems.at[2], bank_v)
    waiting(local_sems.at[3], blocks("q", 4))
    waiting(local_sems.at[4], bank.at[0])
    sub, lane = iota((ROWS, ROWS), 0), iota((ROWS, ROWS), 1)
    upper = (sub <= lane).astype(F32).astype(BF)
    lower = (lane < sub).astype(F32).astype(BF)
    count = counts_v[...].astype(F32)
    count_bf = count.astype(BF)
    ends = nn(count_bf, upper) + jnp.sum(nn(lower, count_bf), axis=1, keepdims=True)
    ends = ends - (m * GROUP).astype(F32)
    starts = ends - count
    inside = (ends > 0.0) & (starts < float(GROUP))
    before = pltpu.roll(count, 1, 1)
    before = jnp.where(lane == 0, pltpu.roll(before, 1, 0), before)
    dd_ref[...] = jnp.where(starts <= 0.0, count, count - before)
    starts = jnp.maximum(starts, 0.0)
    high = jnp.floor(starts * (1.0 / ROWS))
    lo_ref[...] = starts - high * ROWS
    hi_ref[...] = jnp.where(inside, high, 999.0)
    passed = jnp.sum((ends[:, ROWS - 1 :] <= 0.0).astype(F32))
    first = jnp.minimum(passed.astype(jnp.int32), ROWS - WINDOW)
    sub32 = iota((BLOCKS, ROWS), 0).astype(F32)
    subf = sub.astype(F32)

    def scatter(step, total):
        lefts, rights = [], []
        for k in range(2):
            at = pl.ds(first + 2 * step + k, 1)
            same = hi_ref[at, :] == sub32
            mark = jnp.where(same, 1.0, 0.0)
            delta = jnp.where(same, dd_ref[at, :], 0.0)
            lefts.append(jnp.concatenate([mark, delta], axis=0).astype(BF))
            rights.append(jnp.where(lo_ref[at, :] == subf, 1.0, 0.0).astype(BF))
        return total + nt(jnp.concatenate(lefts, axis=1), jnp.concatenate(rights, axis=1))

    marks = lax.fori_loop(0, WINDOW // 2, scatter, jnp.zeros((2 * BLOCKS, ROWS), F32))
    low32 = (iota((BLOCKS, BLOCKS), 1) < iota((BLOCKS, BLOCKS), 0)).astype(F32).astype(BF)

    def running(part):
        part = part.astype(BF)
        return nn(part, upper) + jnp.sum(nn(low32, part), axis=1, keepdims=True)

    reqf[...] = running(marks[:BLOCKS])
    wf[...] = 1.0 / running(marks[BLOCKS:])
    idf[...] = lines_v[0].astype(F32)
    shf[...] = -lines_v[1].astype(F32) * UNIT
    chip_rows = (b, b + 1 - 2 * core)
    for k, at in enumerate(chip_rows):
        rows = pl.ds(k * ROWS, ROWS)
        id_c[rows, :] = as_rows(idf[pl.ds(at, 1), :])
        req_c[rows, :] = as_rows(reqf[pl.ds(at, 1), :])
        sh_c[rows, :] = as_rows(shf[pl.ds(at, 1), :])

    def pair_row(ref, d):
        z_at = lax.rem(z + NZ - d, NZ)
        parts = [ref[pl.ds(x_at * (2 * NZ) + z_at * 2 + core, 1), :] for x_at in (xl, 1 - xl)]
        return jnp.concatenate(parts, axis=1)

    def wide(ref):
        part = ref[...]
        return jnp.concatenate([part, part], axis=1)

    def keep_pair(d):
        keep = (wide(id_c) != pair_row(idf, d)) & (wide(req_c) != pair_row(reqf, d))
        if d == 0:
            keep = keep | (iota((2 * ROWS, 2 * ROWS), 0) == iota((2 * ROWS, 2 * ROWS), 1)) & (
                iota((2 * ROWS, 2 * ROWS), 0) < ROWS
            )
        return keep

    def both(ref):
        return ref[...].reshape(2 * ROWS, DIM)

    def pair(ref, d):
        return ref[2 * d : 2 * d + 2].reshape(2 * ROWS, DIM)

    def row_block(d):
        have("p", d)
        s = TEMP * nt(both(q_chip), pair(p_all, d)) + pair_row(shf, d)
        s = jnp.where(keep_pair(d), s, NEG)
        s_ref[d] = s
        top = jnp.maximum(s[:, :ROWS], s[:, ROWS:])
        mx_ref[...] = top if d == 0 else jnp.maximum(mx_ref[...], top)

    def col_block(d):
        have("q", d)
        t = TEMP * nt(both(p_chip), pair(q_all, d)) + wide(sh_c)
        t_ref[d] = jnp.where(keep_pair(d), t, NEG)

    second("p")
    x_pass("p", 1, 7)
    y_first(1)
    y_first(3)
    z_relay("p", 0)
    y_relay(0)
    x_pass("p", 2, 6)
    y_first(2)
    z_relay("p", 1)
    z_first("q", 0, (2, -2))
    x_first("q")
    x_send("q", 0)
    got("chip", q_chip)
    row_block(0)
    row_block(1)
    row_block(7)
    y_relay(1)
    y_relay(3)
    x_pass("p", 3, 5)
    second("q")
    x_pass("p", 4)
    row_block(2)
    row_block(6)
    y_relay(2)
    x_pass("q", 1, 7)
    z_relay("q", 0)
    x_pass("q", 2, 6)
    row_block(3)
    row_block(5)
    z_relay("q", 1)
    row_block(4)

    row_max = jnp.maximum(jnp.max(mx_ref[...], axis=1, keepdims=True), FLOOR)
    lane_sum = jnp.zeros((2 * ROWS, ROWS), F32)
    for d in range(NZ):
        e = jnp.exp(s_ref[d] - row_max)
        lane_sum = lane_sum + e[:, :ROWS] + e[:, ROWS:]
        e_ref[d] = e.astype(BF)
    row_sum = jnp.sum(lane_sum, axis=1, keepdims=True)
    max_a, sum_a = as_row(row_max[:ROWS]), as_row(row_sum[:ROWS])
    max_p, sum_p = as_row(row_max[ROWS:]), as_row(row_sum[ROWS:])
    stat_out[...] = jnp.where(iota((8, ROWS), 0) == 0, max_p, sum_p)
    send("stat", "stat", stat_out, stat_in, c_dev)

    x_pass("q", 3, 5, 4)
    got("bank", bank.at[pl.ds(0, 5 * NH)])

    q_own = q_chip[0]
    bank_max = None
    for k in range(BANK // ROWS):
        items = bank[4 * k : 4 * k + 4].reshape(ROWS, DIM)
        at = pl.ds(k, 1)
        shift = -bank_v[1, at, :].astype(F32) * UNIT
        keep = (bank_v[0, at, :].astype(F32) != id_c[:ROWS, :]) & (bank_v[2, at, :] < AGE_LIMIT)
        s = jnp.where(keep, TEMP * nt(q_own, items) + shift, NEG)
        sm_ref[k] = s
        bank_max = s if k == 0 else jnp.maximum(bank_max, s)
    max_m = jnp.maximum(jnp.max(bank_max, axis=1, keepdims=True), FLOOR)
    lane_sum = jnp.zeros((ROWS, ROWS), F32)
    for k in range(BANK // ROWS):
        e = jnp.exp(sm_ref[k] - max_m)
        lane_sum = lane_sum + e
        em_ref[:, k * ROWS : (k + 1) * ROWS] = e.astype(BF)
    max_c, sum_c = as_row(max_m), as_row(jnp.sum(lane_sum, axis=1, keepdims=True))

    got("stat", stat_in)
    max_b, sum_b = stat_in[0:1, :], stat_in[1:2, :]
    top = jnp.maximum(jnp.maximum(max_a, max_b), max_c)
    total = sum_a * jnp.exp(max_a - top) + sum_b * jnp.exp(max_b - top) + sum_c * jnp.exp(max_c - top)
    lse = top + jnp.log(total)
    lse_all[0] = jnp.broadcast_to(lse, (8, ROWS))
    for d in (4, 3, 5, 2, 6, 1, 7, 0):
        for col in (1, 0):
            if (col, d) != (0, 0):
                device = on_batch(xl if col == 0 else 1 - xl, lax.rem(z + d, NZ), core)
                send("lse", ("lse", d in (3, 4, 5)), lse_all.at[0], lse_all.at[2 * d + col], device)

    for d in range(NZ):
        part = nn(e_ref[d], pair(p_all, d))
        q_acc[...] = part if d == 0 else q_acc[...] + part
    half_out[...] = q_acc[ROWS:, :]
    send("half", "half", half_out, half_in, c_dev)
    mem_part = nn(em_ref[...], bank[...].reshape(BANK, DIM))

    for d in (0, 1, 7, 2, 6, 3, 5, 4):
        col_block(d)

    for d in (0, 1, 7, 2, 6, 3, 5, 4):
        if d == 0:
            got(("lse", False), lse_all.at[pl.ds(0, 9)])
        if d == 3:
            got(("lse", True), lse_all.at[pl.ds(0, 6)])
        level = jnp.concatenate([lse_all[2 * d][0:1, :], lse_all[2 * d + 1][0:1, :]], axis=1)
        coef = (jnp.exp(t_ref[d] - level) * pair_row(wf, d)).astype(BF)
        part = nn(coef, pair(q_all, d))
        p_acc[...] = part if d == 0 else p_acc[...] + part
    col_out[...] = p_acc[ROWS:, :]
    send("col", "col", col_out, col_in, c_dev)

    weight = wf[pl.ds(b, 1), :]
    scale = TEMP * weight
    fact_a = as_rows(scale * jnp.exp(max_a - lse))[:, 0:1]
    fact_b = as_rows(scale * jnp.exp(max_b - lse))[:, 0:1]
    fact_c = as_rows(scale * jnp.exp(max_c - lse))[:, 0:1]
    own_term = as_rows(scale)[:, 0:1]
    q_f, p_f = q_chip[0].astype(F32), p_chip[0].astype(F32)
    got("half", half_in)
    qgrad_out[...] = (
        fact_a * q_acc[:ROWS, :] + fact_b * half_in[...] + fact_c * mem_part - own_term * p_f
    )
    own_logit = TEMP * as_row(jnp.sum(q_f * p_f, axis=1, keepdims=True)) + shf[pl.ds(b, 1), :]
    loss_out[...] = lse - own_logit
    got("col", col_in)
    pgrad_out[...] = TEMP * (p_acc[:ROWS, :] + col_in[...]) - own_term * q_f

    for out, ref in (
        ("p", blocks("p", 15)), ("q", blocks("q", 15)), ("bank", bank.at[pl.ds(0, 31)]),
        ("lse", lse_all.at[pl.ds(0, 15)]), ("chip", q_chip), ("stat", stat_out), ("half", half_out),
        ("col", col_out),
    ):
        sent(out, ref)


def body(queries, positives, pos_ids, pos_logq, mem_items, mem_ids, mem_logq, mem_age, counts):
    def lines(array):
        return array.reshape(-1, ROWS)

    any_spec = pl.BlockSpec(memory_space=pltpu.HBM)
    vmem_spec = pl.BlockSpec(memory_space=pltpu.VMEM)
    vmem = pltpu.VMEM
    scratch = [
        vmem((2 * NZ, ROWS, DIM), BF),
        vmem((2 * NZ, ROWS, DIM), BF),
        vmem((2, ROWS, DIM), BF),
        vmem((2, ROWS, DIM), BF),
        vmem((BLOCKS, SLOTS, DIM), BF),
        vmem((NZ, 2 * ROWS, 2 * ROWS), F32),
        vmem((NZ, 2 * ROWS, 2 * ROWS), F32),
        vmem((NZ, 2 * ROWS, 2 * ROWS), BF),
        vmem((2 * ROWS, ROWS), F32),
        vmem((ROWS, ROWS), jnp.int32),
        vmem((2, BLOCKS, ROWS), jnp.int32),
        vmem((3, 8, ROWS), jnp.int32),
        vmem((ROWS, ROWS), F32),
        vmem((ROWS, ROWS), F32),
        vmem((ROWS, ROWS), F32),
        vmem((BLOCKS, ROWS), F32),
        vmem((BLOCKS, ROWS), F32),
        vmem((BLOCKS, ROWS), F32),
        vmem((BLOCKS, ROWS), F32),
        vmem((2 * ROWS, ROWS), F32),
        vmem((2 * ROWS, ROWS), F32),
        vmem((2 * ROWS, ROWS), F32),
        vmem((8, ROWS), F32),
        vmem((8, ROWS), F32),
        vmem((2 * NZ, 8, ROWS), F32),
        vmem((ROWS, DIM), F32),
        vmem((ROWS, DIM), F32),
        vmem((ROWS, DIM), F32),
        vmem((ROWS, DIM), F32),
        vmem((2 * ROWS, DIM), F32),
        vmem((2 * ROWS, DIM), F32),
        vmem((BANK // ROWS, ROWS, ROWS), F32),
        vmem((ROWS, BANK), BF),
        pltpu.SemaphoreType.DMA((SENDS,)),
        pltpu.SemaphoreType.DMA((ARRIVALS,)),
        pltpu.SemaphoreType.DMA((LOADS,)),
    ]
    loss, query_grad, positive_grad = pl.pallas_call(
        kernel,
        out_shape=(
            jax.ShapeDtypeStruct((1, ROWS), F32),
            jax.ShapeDtypeStruct((ROWS, DIM), F32),
            jax.ShapeDtypeStruct((ROWS, DIM), F32),
        ),
        in_specs=[any_spec] * 9,
        out_specs=(vmem_spec, vmem_spec, vmem_spec),
        scratch_shapes=scratch,
        compiler_params=pltpu.CompilerParams(
            collective_id=0, has_side_effects=True, vmem_limit_bytes=67043328
        ),
        name="retrieval",
    )(
        queries, positives, mem_items, lines(counts), lines(pos_ids), lines(pos_logq),
        lines(mem_ids), lines(mem_logq), lines(mem_age),
    )
    return loss.reshape(ROWS), query_grad, positive_grad


def solution(mesh):
    in_specs = (
        P(("mem", "batch"), None),
        P(("mem", "batch"), None),
        P(),
        P(),
        P(("batch", "mem"), None),
        P(),
        P(),
        P(),
        P(),
    )
    out_specs = (P(("mem", "batch")), P(("mem", "batch"), None), P(("mem", "batch"), None))
    return jax.shard_map(body, mesh=mesh, in_specs=in_specs, out_specs=out_specs, check_vma=False)
```

```python
import jax
import jax.numpy as jnp
from jax import lax
from jax.experimental import pallas as pl
from jax.experimental.pallas import tpu as pltpu
from jax.sharding import PartitionSpec as P

MESH = pl.DeviceIdType.MESH
AGE_LIMIT = 16
NZ, NY, NH = 8, 8, 4
ROWS, DIM, CUT = 128, 256, 32
BLOCKS = 32
GROUP = ROWS * BLOCKS
SLOTS = 32
BANK = 1024
WINDOW = 34
TEMP = 8.0
UNIT = 1.0 / 1024.0
NEG = -1e30
FLOOR = -1e20
SENDS, ARRIVALS, LOADS = 8, 42, 5
BF, F32 = jnp.bfloat16, jnp.float32


def nt(left, right):
    return lax.dot_general(left, right, (((1,), (1,)), ((), ())), preferred_element_type=F32)


def nn(left, right):
    return lax.dot_general(left, right, (((1,), (0,)), ((), ())), preferred_element_type=F32)


def iota(shape, dim):
    return lax.broadcasted_iota(jnp.int32, shape, dim)


def as_rows(row):
    return jnp.broadcast_to(row, (ROWS, ROWS)).T


def as_row(column):
    return jnp.broadcast_to(column, (ROWS, ROWS)).T[0:1, :]


def kernel(
    q_hbm, p_hbm, items_hbm, counts_hbm, ids_hbm, logq_hbm, bids_hbm, blogq_hbm, bage_hbm,
    loss_out, qgrad_out, pgrad_out,
    q_all, p_all, q_chip, p_chip, bank,
    s_ref, t_ref, e_ref, mx_ref,
    counts_v, lines_v, bank_v,
    hi_ref, lo_ref, dd_ref, idf, reqf, shf, wf, id_c, req_c, sh_c,
    stat_out, stat_in, lse_all, half_out, half_in, col_out, col_in, q_acc, p_acc,
    sm_ref, em_ref,
    send_sems, recv_sems, local_sems,
):
    b = lax.axis_index("batch")
    m = lax.axis_index("mem")
    core = lax.rem(b, 2)
    z = lax.rem(lax.div(b, 2), NZ)
    xl = lax.div(b, 2 * NZ)
    y = lax.rem(m, NY)
    xh = lax.div(m, NY)

    def on_batch(x_at, z_at, core_at):
        return {"batch": x_at * (2 * NZ) + z_at * 2 + core_at, "mem": m}

    def on_mem(h_at, y_at):
        return {"batch": b, "mem": h_at * NY + y_at}

    def z_dev(hop):
        return on_batch(xl, lax.rem(z + hop + NZ, NZ), core)

    def y_dev(hop):
        return on_mem(xh, lax.rem(y + hop + NY, NY))

    x_dev = on_batch(1 - xl, z, core)
    c_dev = on_batch(xl, z, 1 - core)
    h_dev = {e: on_mem(lax.rem(xh + e, NH), y) for e in (1, 3)}

    send_at, arrive_at = {}, {}

    def send(out, into, src, dst, device):
        pltpu.make_async_remote_copy(
            src_ref=src,
            dst_ref=dst,
            send_sem=send_sems.at[send_at.setdefault(out, len(send_at))],
            recv_sem=recv_sems.at[arrive_at.setdefault(into, len(arrive_at))],
            device_id=device,
            device_id_type=MESH,
        ).start()

    def waiting(sem, ref):
        pltpu.make_async_copy(ref, ref, sem).wait()

    def sent(out, ref):
        waiting(send_sems.at[send_at[out]], ref)

    def got(into, ref):
        waiting(recv_sems.at[arrive_at[into]], ref)

    def load(kind, src, dst):
        pltpu.make_async_copy(src, dst, local_sems.at[kind]).start()

    load(0, counts_hbm, counts_v)
    load(1, ids_hbm.at[pl.ds(m * BLOCKS, BLOCKS)], lines_v.at[0])
    load(1, logq_hbm.at[pl.ds(m * BLOCKS, BLOCKS)], lines_v.at[1])
    load(2, bids_hbm.at[pl.ds(b * 8, 8)], bank_v.at[0])
    load(2, blogq_hbm.at[pl.ds(b * 8, 8)], bank_v.at[1])
    load(2, bage_hbm.at[pl.ds(b * 8, 8)], bank_v.at[2])
    load(3, q_hbm, q_all.at[0])
    load(3, p_hbm, p_all.at[0])
    load(3, q_hbm, q_chip.at[0])
    load(3, p_hbm, p_chip.at[0])
    load(4, items_hbm, bank.at[m])

    def requests():
        waiting(local_sems.at[0], counts_v)
        waiting(local_sems.at[1], lines_v)
        sub, lane = iota((ROWS, ROWS), 0), iota((ROWS, ROWS), 1)
        upper = (sub <= lane).astype(F32).astype(BF)
        lower = (lane < sub).astype(F32).astype(BF)
        count = counts_v[...].astype(F32)
        count_bf = count.astype(BF)
        ends = nn(count_bf, upper) + jnp.sum(nn(lower, count_bf), axis=1, keepdims=True)
        ends = ends - (m * GROUP).astype(F32)
        starts = ends - count
        inside = (ends > 0.0) & (starts < float(GROUP))
        before = pltpu.roll(count, 1, 1)
        before = jnp.where(lane == 0, pltpu.roll(before, 1, 0), before)
        dd_ref[...] = jnp.where(starts <= 0.0, count, count - before)
        starts = jnp.maximum(starts, 0.0)
        high = jnp.floor(starts * (1.0 / ROWS))
        lo_ref[...] = starts - high * ROWS
        hi_ref[...] = jnp.where(inside, high, 999.0)
        passed = jnp.sum((ends[:, ROWS - 1 :] <= 0.0).astype(F32))
        first = jnp.minimum(passed.astype(jnp.int32), ROWS - WINDOW)
        sub32 = iota((BLOCKS, ROWS), 0).astype(F32)
        subf = sub.astype(F32)

        def scatter(step, total):
            lefts, rights = [], []
            for k in range(2):
                at = pl.ds(first + 2 * step + k, 1)
                same = hi_ref[at, :] == sub32
                mark = jnp.where(same, 1.0, 0.0)
                delta = jnp.where(same, dd_ref[at, :], 0.0)
                lefts.append(jnp.concatenate([mark, delta], axis=0).astype(BF))
                rights.append(jnp.where(lo_ref[at, :] == subf, 1.0, 0.0).astype(BF))
            return total + nt(jnp.concatenate(lefts, axis=1), jnp.concatenate(rights, axis=1))

        marks = lax.fori_loop(0, WINDOW // 2, scatter, jnp.zeros((2 * BLOCKS, ROWS), F32))
        low32 = (iota((BLOCKS, BLOCKS), 1) < iota((BLOCKS, BLOCKS), 0)).astype(F32).astype(BF)

        def running(part):
            part = part.astype(BF)
            return nn(part, upper) + jnp.sum(nn(low32, part), axis=1, keepdims=True)

        reqf[...] = running(marks[:BLOCKS])
        wf[...] = 1.0 / running(marks[BLOCKS:])
        idf[...] = lines_v[0].astype(F32)
        shf[...] = -lines_v[1].astype(F32) * UNIT
        chip_rows = (b, b + 1 - 2 * core)
        for k, at in enumerate(chip_rows):
            rows = pl.ds(k * ROWS, ROWS)
            id_c[rows, :] = as_rows(idf[pl.ds(at, 1), :])
            req_c[rows, :] = as_rows(reqf[pl.ds(at, 1), :])
            sh_c[rows, :] = as_rows(shf[pl.ds(at, 1), :])

    barrier = pltpu.get_barrier_semaphore()
    near = [place(hop) for place in (z_dev, y_dev) for hop in (1, -1, 2, -2)]
    near += [x_dev, c_dev, h_dev[1], h_dev[3]]
    for device in near:
        pl.semaphore_signal(barrier, inc=1, device_id=device, device_id_type=MESH)
    pl.when(z < 6)(requests)
    pl.semaphore_wait(barrier, len(near))

    own = {"q": q_hbm, "p": p_hbm}
    held = {"q": q_all, "p": p_all}
    onward = {"p": ((2, 1), (2, 2), (6, -1)), "q": ((2, 1), (6, -1), (6, -2))}

    def blocks(arr, n):
        return held[arr].at[pl.ds(0, n)]

    def piece(arr, col, d):
        if col == 0 and d == 0:
            return own[arr]
        return held[arr].at[2 * d] if col == 0 else held[arr].at[2 * d + 1, pl.ds(0, CUT)]

    final = {1: "near", 7: "near", 3: "far", 5: "far", 4: "last"}

    def z_send(arr, col, d, hop):
        there = (d + hop) % NZ
        block = held[arr].at[2 * there + col]
        dst = block if col == 0 else held[arr].at[2 * there + 1, pl.ds(0, CUT)]
        into = there if col == 0 else final.get(there, "cut")
        send(arr, (arr, into), piece(arr, col, d), dst, z_dev(hop))

    def z_first(arr, col, hops):
        for hop in hops:
            z_send(arr, col, 0, hop)

    def side(arr, near, far):
        got((arr, near), blocks(arr, 1))
        x_send(arr, near)
        got((arr, far), blocks(arr, 1))
        for d, hop in onward[arr]:
            if d == far:
                z_send(arr, 0, d, hop)
        x_send(arr, far)

    def cut_relay(arr):
        got((arr, "cut"), held[arr].at[1, pl.ds(0, 2 * CUT)])
        for d, hop in onward[arr]:
            z_send(arr, 1, d, hop)

    def x_first(arr):
        src, dst = own[arr].at[pl.ds(0, CUT)], held[arr].at[1, pl.ds(0, CUT)]
        send(arr, (arr, "first"), src, dst, x_dev)

    def x_send(arr, d):
        rest = pl.ds(CUT, ROWS - CUT)
        src = own[arr].at[rest] if d == 0 else held[arr].at[2 * d, rest]
        into = final.get(d, "x0" if d == 0 else "x2")
        send(arr, (arr, into), src, held[arr].at[2 * d + 1, rest], x_dev)

    def x_pass(arr, *group):
        for d in group:
            got((arr, d), blocks(arr, 1))
            x_send(arr, d)

    def second(arr):
        got((arr, "first"), held[arr].at[1, pl.ds(0, CUT)])
        z_first(arr, 1, (1, -1, 2, -2))

    def have(arr, d):
        rest = ROWS - CUT
        if d == 0:
            got((arr, "x0"), held[arr].at[1, pl.ds(0, rest)])
        if d == 2:
            got((arr, "x2"), held[arr].at[pl.ds(0, 2), pl.ds(0, rest)])
        if d in (1, 3):
            got((arr, final[d]), blocks(arr, 2))
        if d == 4:
            got((arr, final[d]), blocks(arr, 1))

    def bank_at(e, dy):
        return lax.rem(xh + NH - e, NH) * NY + lax.rem(y + NY - dy, NY)

    def y_send(e, d, hop):
        at, there = bank_at(e, d), (d + hop) % NY
        src = items_hbm if (e, d) == (0, 0) else bank.at[at]
        into = ("bank", e) if there in (2, 6) else "bank"
        send("bank", into, src, bank.at[at], y_dev(hop))

    def y_first(e):
        if e:
            got(("h", e), bank.at[0])
        if e == 1:
            send("bank", ("h", 2), bank.at[bank_at(1, 0)], bank.at[bank_at(1, 0)], h_dev[1])
        for hop in (1, -1, 2, -2):
            y_send(e, 0, hop)

    def y_relay(e):
        got(("bank", e), bank.at[pl.ds(0, 2)])
        for d, hop in ((2, 1), (2, 2), (6, -1)) if e in (0, 1) else ((2, 1), (6, -1), (6, -2)):
            y_send(e, d, hop)

    z_first("p", 0, (2, -2, 1, -1))
    x_first("p")
    for e in (1, 3):
        send("bank", ("h", e), items_hbm, bank.at[m], h_dev[e])
    y_first(0)
    x_send("p", 0)
    send("chip", "chip", q_hbm, q_chip.at[1], c_dev)
    send("chip", "chip", p_hbm, p_chip.at[1], c_dev)
    waiting(local_sems.at[2], bank_v)
    waiting(local_sems.at[3], blocks("q", 4))
    waiting(local_sems.at[4], bank.at[0])

    def pair_row(ref, d):
        z_at = lax.rem(z + NZ - d, NZ)
        parts = [ref[pl.ds(x_at * (2 * NZ) + z_at * 2 + core, 1), :] for x_at in (xl, 1 - xl)]
        return jnp.concatenate(parts, axis=1)

    def wide(ref):
        part = ref[...]
        return jnp.concatenate([part, part], axis=1)

    def keep_pair(d):
        keep = (wide(id_c) != pair_row(idf, d)) & (wide(req_c) != pair_row(reqf, d))
        if d == 0:
            keep = keep | (iota((2 * ROWS, 2 * ROWS), 0) == iota((2 * ROWS, 2 * ROWS), 1)) & (
                iota((2 * ROWS, 2 * ROWS), 0) < ROWS
            )
        return keep

    def both(ref):
        return ref[...].reshape(2 * ROWS, DIM)

    def pair(ref, d):
        return ref[2 * d : 2 * d + 2].reshape(2 * ROWS, DIM)

    def row_block(d):
        have("p", d)
        s = TEMP * nt(both(q_chip), pair(p_all, d)) + pair_row(shf, d)
        s = jnp.where(keep_pair(d), s, NEG)
        s_ref[d] = s
        top = jnp.maximum(s[:, :ROWS], s[:, ROWS:])
        mx_ref[...] = top if d == 0 else jnp.maximum(mx_ref[...], top)

    def col_block(d):
        have("q", d)
        t = TEMP * nt(both(p_chip), pair(q_all, d)) + wide(sh_c)
        t_ref[d] = jnp.where(keep_pair(d), t, NEG)

    pl.when(z < 2)(lambda: side("p", 7, 6))
    pl.when(z >= 2)(lambda: side("p", 1, 2))
    second("p")
    y_first(1)
    y_first(3)
    z_first("q", 0, (1, -1))
    pl.when(z < 2)(lambda: side("p", 1, 2))
    pl.when(z >= 2)(lambda: side("p", 7, 6))
    y_relay(0)
    y_first(2)
    cut_relay("p")
    z_first("q", 0, (2, -2))
    x_first("q")
    x_send("q", 0)
    got("chip", q_chip)
    pl.when(z >= 6)(requests)
    row_block(0)
    x_pass("p", 3, 5, 4)
    row_block(1)
    row_block(7)
    second("q")
    y_relay(1)
    y_relay(3)
    row_block(2)
    row_block(6)
    side("q", 1, 2)
    side("q", 7, 6)
    y_relay(2)
    row_block(3)
    row_block(5)
    row_block(4)
    cut_relay("q")

    row_max = jnp.maximum(jnp.max(mx_ref[...], axis=1, keepdims=True), FLOOR)
    lane_sum = jnp.zeros((2 * ROWS, ROWS), F32)
    for d in range(NZ):
        e = jnp.exp(s_ref[d] - row_max)
        lane_sum = lane_sum + e[:, :ROWS] + e[:, ROWS:]
        e_ref[d] = e.astype(BF)
    row_sum = jnp.sum(lane_sum, axis=1, keepdims=True)
    max_a, sum_a = as_row(row_max[:ROWS]), as_row(row_sum[:ROWS])
    max_p, sum_p = as_row(row_max[ROWS:]), as_row(row_sum[ROWS:])
    stat_out[...] = jnp.where(iota((8, ROWS), 0) == 0, max_p, sum_p)
    send("stat", "stat", stat_out, stat_in, c_dev)

    x_pass("q", 3, 5, 4)
    got("bank", bank.at[pl.ds(0, 5 * NH)])

    q_own = q_chip[0]
    bank_max = None
    for k in range(BANK // ROWS):
        items = bank[4 * k : 4 * k + 4].reshape(ROWS, DIM)
        at = pl.ds(k, 1)
        shift = -bank_v[1, at, :].astype(F32) * UNIT
        keep = (bank_v[0, at, :].astype(F32) != id_c[:ROWS, :]) & (bank_v[2, at, :] < AGE_LIMIT)
        s = jnp.where(keep, TEMP * nt(q_own, items) + shift, NEG)
        sm_ref[k] = s
        bank_max = s if k == 0 else jnp.maximum(bank_max, s)
    max_m = jnp.maximum(jnp.max(bank_max, axis=1, keepdims=True), FLOOR)
    lane_sum = jnp.zeros((ROWS, ROWS), F32)
    for k in range(BANK // ROWS):
        e = jnp.exp(sm_ref[k] - max_m)
        lane_sum = lane_sum + e
        em_ref[:, k * ROWS : (k + 1) * ROWS] = e.astype(BF)
    max_c, sum_c = as_row(max_m), as_row(jnp.sum(lane_sum, axis=1, keepdims=True))

    got("stat", stat_in)
    max_b, sum_b = stat_in[0:1, :], stat_in[1:2, :]
    top = jnp.maximum(jnp.maximum(max_a, max_b), max_c)
    total = sum_a * jnp.exp(max_a - top) + sum_b * jnp.exp(max_b - top) + sum_c * jnp.exp(max_c - top)
    lse = top + jnp.log(total)
    lse_all[0] = jnp.broadcast_to(lse, (8, ROWS))
    for d in (4, 3, 5, 2, 6, 1, 7, 0):
        for col in (1, 0):
            if (col, d) != (0, 0):
                device = on_batch(xl if col == 0 else 1 - xl, lax.rem(z + d, NZ), core)
                send("lse", ("lse", d in (3, 4, 5)), lse_all.at[0], lse_all.at[2 * d + col], device)

    for d in range(NZ):
        part = nn(e_ref[d], pair(p_all, d))
        q_acc[...] = part if d == 0 else q_acc[...] + part
    half_out[...] = q_acc[ROWS:, :]
    send("half", "half", half_out, half_in, c_dev)
    mem_part = nn(em_ref[...], bank[...].reshape(BANK, DIM))

    for d in (0, 1, 7, 2, 6, 3, 5, 4):
        col_block(d)

    for d in (0, 1, 7, 2, 6, 3, 5, 4):
        if d == 0:
            got(("lse", False), lse_all.at[pl.ds(0, 9)])
        if d == 3:
            got(("lse", True), lse_all.at[pl.ds(0, 6)])
        level = jnp.concatenate([lse_all[2 * d][0:1, :], lse_all[2 * d + 1][0:1, :]], axis=1)
        coef = (jnp.exp(t_ref[d] - level) * pair_row(wf, d)).astype(BF)
        part = nn(coef, pair(q_all, d))
        p_acc[...] = part if d == 0 else p_acc[...] + part
    col_out[...] = p_acc[ROWS:, :]
    send("col", "col", col_out, col_in, c_dev)

    weight = wf[pl.ds(b, 1), :]
    scale = TEMP * weight
    fact_a = as_rows(scale * jnp.exp(max_a - lse))[:, 0:1]
    fact_b = as_rows(scale * jnp.exp(max_b - lse))[:, 0:1]
    fact_c = as_rows(scale * jnp.exp(max_c - lse))[:, 0:1]
    own_term = as_rows(scale)[:, 0:1]
    q_f, p_f = q_chip[0].astype(F32), p_chip[0].astype(F32)
    got("half", half_in)
    qgrad_out[...] = (
        fact_a * q_acc[:ROWS, :] + fact_b * half_in[...] + fact_c * mem_part - own_term * p_f
    )
    own_logit = TEMP * as_row(jnp.sum(q_f * p_f, axis=1, keepdims=True)) + shf[pl.ds(b, 1), :]
    loss_out[...] = lse - own_logit
    got("col", col_in)
    pgrad_out[...] = TEMP * (p_acc[:ROWS, :] + col_in[...]) - own_term * q_f

    assert (len(send_at), len(arrive_at)) == (SENDS, ARRIVALS)
    for out, ref in (
        ("p", blocks("p", 15)), ("q", blocks("q", 15)), ("bank", bank.at[pl.ds(0, 31)]),
        ("lse", lse_all.at[pl.ds(0, 15)]), ("chip", q_chip), ("stat", stat_out), ("half", half_out),
        ("col", col_out),
    ):
        sent(out, ref)


def body(queries, positives, pos_ids, pos_logq, mem_items, mem_ids, mem_logq, mem_age, counts):
    def lines(array):
        return array.reshape(-1, ROWS)

    any_spec = pl.BlockSpec(memory_space=pltpu.HBM)
    vmem_spec = pl.BlockSpec(memory_space=pltpu.VMEM)
    vmem = pltpu.VMEM
    scratch = [
        vmem((2 * NZ, ROWS, DIM), BF),
        vmem((2 * NZ, ROWS, DIM), BF),
        vmem((2, ROWS, DIM), BF),
        vmem((2, ROWS, DIM), BF),
        vmem((BLOCKS, SLOTS, DIM), BF),
        vmem((NZ, 2 * ROWS, 2 * ROWS), F32),
        vmem((NZ, 2 * ROWS, 2 * ROWS), F32),
        vmem((NZ, 2 * ROWS, 2 * ROWS), BF),
        vmem((2 * ROWS, ROWS), F32),
        vmem((ROWS, ROWS), jnp.int32),
        vmem((2, BLOCKS, ROWS), jnp.int32),
        vmem((3, 8, ROWS), jnp.int32),
        vmem((ROWS, ROWS), F32),
        vmem((ROWS, ROWS), F32),
        vmem((ROWS, ROWS), F32),
        vmem((BLOCKS, ROWS), F32),
        vmem((BLOCKS, ROWS), F32),
        vmem((BLOCKS, ROWS), F32),
        vmem((BLOCKS, ROWS), F32),
        vmem((2 * ROWS, ROWS), F32),
        vmem((2 * ROWS, ROWS), F32),
        vmem((2 * ROWS, ROWS), F32),
        vmem((8, ROWS), F32),
        vmem((8, ROWS), F32),
        vmem((2 * NZ, 8, ROWS), F32),
        vmem((ROWS, DIM), F32),
        vmem((ROWS, DIM), F32),
        vmem((ROWS, DIM), F32),
        vmem((ROWS, DIM), F32),
        vmem((2 * ROWS, DIM), F32),
        vmem((2 * ROWS, DIM), F32),
        vmem((BANK // ROWS, ROWS, ROWS), F32),
        vmem((ROWS, BANK), BF),
        pltpu.SemaphoreType.DMA((SENDS,)),
        pltpu.SemaphoreType.DMA((ARRIVALS,)),
        pltpu.SemaphoreType.DMA((LOADS,)),
    ]
    loss, query_grad, positive_grad = pl.pallas_call(
        kernel,
        out_shape=(
            jax.ShapeDtypeStruct((1, ROWS), F32),
            jax.ShapeDtypeStruct((ROWS, DIM), F32),
            jax.ShapeDtypeStruct((ROWS, DIM), F32),
        ),
        in_specs=[any_spec] * 9,
        out_specs=(vmem_spec, vmem_spec, vmem_spec),
        scratch_shapes=scratch,
        compiler_params=pltpu.CompilerParams(
            collective_id=0, has_side_effects=True, vmem_limit_bytes=67043328
        ),
        name="retrieval",
    )(
        queries, positives, mem_items, lines(counts), lines(pos_ids), lines(pos_logq),
        lines(mem_ids), lines(mem_logq), lines(mem_age),
    )
    return loss.reshape(ROWS), query_grad, positive_grad


def solution(mesh):
    in_specs = (
        P(("mem", "batch"), None),
        P(("mem", "batch"), None),
        P(),
        P(),
        P(("batch", "mem"), None),
        P(),
        P(),
        P(),
        P(),
    )
    out_specs = (P(("mem", "batch")), P(("mem", "batch"), None), P(("mem", "batch"), None))
    return jax.shard_map(body, mesh=mesh, in_specs=in_specs, out_specs=out_specs, check_vma=False)
```

```python
import jax
import jax.numpy as jnp
from jax import lax
from jax.experimental import pallas as pl
from jax.experimental.pallas import tpu as pltpu
from jax.sharding import PartitionSpec as P

MESH = pl.DeviceIdType.MESH
AGE_LIMIT = 16
NZ, NY, NH = 8, 8, 4
ROWS, DIM, CUT = 128, 256, 32
BLOCKS = 32
GROUP = ROWS * BLOCKS
SLOTS = 32
BANK = 1024
WINDOW = 34
TEMP = 8.0
UNIT = 1.0 / 1024.0
NEG = -1e30
FLOOR = -1e20
SENDS, ARRIVALS, LOADS = 8, 42, 5
BF, F32 = jnp.bfloat16, jnp.float32


def nt(left, right):
    return lax.dot_general(left, right, (((1,), (1,)), ((), ())), preferred_element_type=F32)


def nn(left, right):
    return lax.dot_general(left, right, (((1,), (0,)), ((), ())), preferred_element_type=F32)


def iota(shape, dim):
    return lax.broadcasted_iota(jnp.int32, shape, dim)


def as_rows(row):
    return jnp.broadcast_to(row, (ROWS, ROWS)).T


def as_row(column):
    return jnp.broadcast_to(column, (ROWS, ROWS)).T[0:1, :]


def kernel(
    q_hbm, p_hbm, items_hbm, counts_hbm, ids_hbm, logq_hbm, bids_hbm, blogq_hbm, bage_hbm,
    loss_out, qgrad_out, pgrad_out,
    q_all, p_all, q_chip, p_chip, bank,
    s_ref, t_ref, e_ref, mx_ref,
    counts_v, lines_v, bank_v,
    hi_ref, lo_ref, dd_ref, idf, reqf, shf, wf, id_c, req_c, sh_c,
    stat_out, stat_in, lse_all, half_out, half_in, col_out, col_in, q_acc, p_acc,
    sm_ref, em_ref,
    send_sems, recv_sems, local_sems,
):
    b = lax.axis_index("batch")
    m = lax.axis_index("mem")
    core = lax.rem(b, 2)
    z = lax.rem(lax.div(b, 2), NZ)
    xl = lax.div(b, 2 * NZ)
    y = lax.rem(m, NY)
    xh = lax.div(m, NY)

    def on_batch(x_at, z_at, core_at):
        return {"batch": x_at * (2 * NZ) + z_at * 2 + core_at, "mem": m}

    def on_mem(h_at, y_at):
        return {"batch": b, "mem": h_at * NY + y_at}

    def z_dev(hop):
        return on_batch(xl, lax.rem(z + hop + NZ, NZ), core)

    def y_dev(hop):
        return on_mem(xh, lax.rem(y + hop + NY, NY))

    x_dev = on_batch(1 - xl, z, core)
    c_dev = on_batch(xl, z, 1 - core)
    h_dev = {e: on_mem(lax.rem(xh + e, NH), y) for e in (1, 3)}

    send_at, arrive_at = {}, {}

    def send(out, into, src, dst, device):
        pltpu.make_async_remote_copy(
            src_ref=src,
            dst_ref=dst,
            send_sem=send_sems.at[send_at.setdefault(out, len(send_at))],
            recv_sem=recv_sems.at[arrive_at.setdefault(into, len(arrive_at))],
            device_id=device,
            device_id_type=MESH,
        ).start()

    def waiting(sem, ref):
        pltpu.make_async_copy(ref, ref, sem).wait()

    def sent(out, ref):
        waiting(send_sems.at[send_at[out]], ref)

    def got(into, ref):
        waiting(recv_sems.at[arrive_at[into]], ref)

    def load(kind, src, dst):
        pltpu.make_async_copy(src, dst, local_sems.at[kind]).start()

    load(0, counts_hbm, counts_v)
    load(1, ids_hbm.at[pl.ds(m * BLOCKS, BLOCKS)], lines_v.at[0])
    load(1, logq_hbm.at[pl.ds(m * BLOCKS, BLOCKS)], lines_v.at[1])
    load(2, bids_hbm.at[pl.ds(b * 8, 8)], bank_v.at[0])
    load(2, blogq_hbm.at[pl.ds(b * 8, 8)], bank_v.at[1])
    load(2, bage_hbm.at[pl.ds(b * 8, 8)], bank_v.at[2])
    load(3, q_hbm, q_all.at[0])
    load(3, p_hbm, p_all.at[0])
    load(3, q_hbm, q_chip.at[0])
    load(3, p_hbm, p_chip.at[0])
    load(4, items_hbm, bank.at[m])

    def requests():
        waiting(local_sems.at[0], counts_v)
        waiting(local_sems.at[1], lines_v)
        sub, lane = iota((ROWS, ROWS), 0), iota((ROWS, ROWS), 1)
        upper = (sub <= lane).astype(F32).astype(BF)
        lower = (lane < sub).astype(F32).astype(BF)
        count = counts_v[...].astype(F32)
        count_bf = count.astype(BF)
        ends = nn(count_bf, upper) + jnp.sum(nn(lower, count_bf), axis=1, keepdims=True)
        ends = ends - (m * GROUP).astype(F32)
        starts = ends - count
        inside = (ends > 0.0) & (starts < float(GROUP))
        before = pltpu.roll(count, 1, 1)
        before = jnp.where(lane == 0, pltpu.roll(before, 1, 0), before)
        dd_ref[...] = jnp.where(starts <= 0.0, count, count - before)
        starts = jnp.maximum(starts, 0.0)
        high = jnp.floor(starts * (1.0 / ROWS))
        lo_ref[...] = starts - high * ROWS
        hi_ref[...] = jnp.where(inside, high, 999.0)
        passed = jnp.sum((ends[:, ROWS - 1 :] <= 0.0).astype(F32))
        first = jnp.minimum(passed.astype(jnp.int32), ROWS - WINDOW)
        sub32 = iota((BLOCKS, ROWS), 0).astype(F32)
        subf = sub.astype(F32)

        def scatter(step, total):
            lefts, rights = [], []
            for k in range(2):
                at = pl.ds(first + 2 * step + k, 1)
                same = hi_ref[at, :] == sub32
                mark = jnp.where(same, 1.0, 0.0)
                delta = jnp.where(same, dd_ref[at, :], 0.0)
                lefts.append(jnp.concatenate([mark, delta], axis=0).astype(BF))
                rights.append(jnp.where(lo_ref[at, :] == subf, 1.0, 0.0).astype(BF))
            return total + nt(jnp.concatenate(lefts, axis=1), jnp.concatenate(rights, axis=1))

        marks = lax.fori_loop(0, WINDOW // 2, scatter, jnp.zeros((2 * BLOCKS, ROWS), F32))
        low32 = (iota((BLOCKS, BLOCKS), 1) < iota((BLOCKS, BLOCKS), 0)).astype(F32).astype(BF)

        def running(part):
            part = part.astype(BF)
            return nn(part, upper) + jnp.sum(nn(low32, part), axis=1, keepdims=True)

        reqf[...] = running(marks[:BLOCKS])
        wf[...] = 1.0 / running(marks[BLOCKS:])
        idf[...] = lines_v[0].astype(F32)
        shf[...] = -lines_v[1].astype(F32) * UNIT
        chip_rows = (b, b + 1 - 2 * core)
        for k, at in enumerate(chip_rows):
            rows = pl.ds(k * ROWS, ROWS)
            id_c[rows, :] = as_rows(idf[pl.ds(at, 1), :])
            req_c[rows, :] = as_rows(reqf[pl.ds(at, 1), :])
            sh_c[rows, :] = as_rows(shf[pl.ds(at, 1), :])

    barrier = pltpu.get_barrier_semaphore()
    near = [place(hop) for place in (z_dev, y_dev) for hop in (1, -1, 2, -2)]
    near += [x_dev, c_dev, h_dev[1], h_dev[3]]
    for device in near:
        pl.semaphore_signal(barrier, inc=1, device_id=device, device_id_type=MESH)
    pl.when(z < 6)(requests)
    pl.semaphore_wait(barrier, len(near))

    own = {"q": q_hbm, "p": p_hbm}
    held = {"q": q_all, "p": p_all}
    onward = {"p": ((2, 1), (2, 2), (6, -1)), "q": ((2, 1), (6, -1), (6, -2))}

    def blocks(arr, n):
        return held[arr].at[pl.ds(0, n)]

    def piece(arr, col, d):
        if col == 0 and d == 0:
            return own[arr]
        return held[arr].at[2 * d] if col == 0 else held[arr].at[2 * d + 1, pl.ds(0, CUT)]

    final = {1: "near", 7: "near", 3: "far", 5: "far", 4: "last"}

    def z_send(arr, col, d, hop):
        there = (d + hop) % NZ
        block = held[arr].at[2 * there + col]
        dst = block if col == 0 else held[arr].at[2 * there + 1, pl.ds(0, CUT)]
        into = there if col == 0 else final.get(there, "cut")
        send(arr, (arr, into), piece(arr, col, d), dst, z_dev(hop))

    def z_first(arr, col, hops):
        for hop in hops:
            z_send(arr, col, 0, hop)

    def side(arr, near, far):
        got((arr, near), blocks(arr, 1))
        x_send(arr, near)
        got((arr, far), blocks(arr, 1))
        for d, hop in onward[arr]:
            if d == far:
                z_send(arr, 0, d, hop)
        x_send(arr, far)

    def cut_relay(arr):
        got((arr, "cut"), held[arr].at[1, pl.ds(0, 2 * CUT)])
        for d, hop in onward[arr]:
            z_send(arr, 1, d, hop)

    def x_first(arr):
        src, dst = own[arr].at[pl.ds(0, CUT)], held[arr].at[1, pl.ds(0, CUT)]
        send(arr, (arr, "first"), src, dst, x_dev)

    def x_send(arr, d):
        rest = pl.ds(CUT, ROWS - CUT)
        src = own[arr].at[rest] if d == 0 else held[arr].at[2 * d, rest]
        into = final.get(d, "x0" if d == 0 else "x2")
        send(arr, (arr, into), src, held[arr].at[2 * d + 1, rest], x_dev)

    def x_pass(arr, *group):
        for d in group:
            got((arr, d), blocks(arr, 1))
            x_send(arr, d)

    def second(arr):
        got((arr, "first"), held[arr].at[1, pl.ds(0, CUT)])
        z_first(arr, 1, (1, -1, 2, -2))

    def have(arr, d):
        rest = ROWS - CUT
        if d == 0:
            got((arr, "x0"), held[arr].at[1, pl.ds(0, rest)])
        if d == 2:
            got((arr, "x2"), held[arr].at[pl.ds(0, 2), pl.ds(0, rest)])
        if d in (1, 3):
            got((arr, final[d]), blocks(arr, 2))
        if d == 4:
            got((arr, final[d]), blocks(arr, 1))

    def bank_at(e, dy):
        return lax.rem(xh + NH - e, NH) * NY + lax.rem(y + NY - dy, NY)

    def y_send(e, d, hop):
        at, there = bank_at(e, d), (d + hop) % NY
        src = items_hbm if (e, d) == (0, 0) else bank.at[at]
        into = ("bank", e) if there in (2, 6) else "bank"
        send("bank", into, src, bank.at[at], y_dev(hop))

    def y_first(e):
        if e:
            got(("h", e), bank.at[0])
        if e == 1:
            send("bank", ("h", 2), bank.at[bank_at(1, 0)], bank.at[bank_at(1, 0)], h_dev[1])
        for hop in (1, -1, 2, -2):
            y_send(e, 0, hop)

    def y_relay(e):
        got(("bank", e), bank.at[pl.ds(0, 2)])
        for d, hop in ((2, 1), (2, 2), (6, -1)) if e in (0, 1) else ((2, 1), (6, -1), (6, -2)):
            y_send(e, d, hop)

    z_first("p", 0, (2, -2, 1, -1))
    x_first("p")
    for e in (1, 3):
        send("bank", ("h", e), items_hbm, bank.at[m], h_dev[e])
    y_first(0)
    x_send("p", 0)
    send("chip", "chip", q_hbm, q_chip.at[1], c_dev)
    send("chip", "chip", p_hbm, p_chip.at[1], c_dev)
    waiting(local_sems.at[2], bank_v)
    waiting(local_sems.at[3], blocks("q", 4))
    waiting(local_sems.at[4], bank.at[0])

    def pair_row(ref, d):
        z_at = lax.rem(z + NZ - d, NZ)
        parts = [ref[pl.ds(x_at * (2 * NZ) + z_at * 2 + core, 1), :] for x_at in (xl, 1 - xl)]
        return jnp.concatenate(parts, axis=1)

    def wide(ref):
        part = ref[...]
        return jnp.concatenate([part, part], axis=1)

    def keep_pair(d):
        keep = (wide(id_c) != pair_row(idf, d)) & (wide(req_c) != pair_row(reqf, d))
        if d == 0:
            keep = keep | (iota((2 * ROWS, 2 * ROWS), 0) == iota((2 * ROWS, 2 * ROWS), 1)) & (
                iota((2 * ROWS, 2 * ROWS), 0) < ROWS
            )
        return keep

    def both(ref):
        return ref[...].reshape(2 * ROWS, DIM)

    def pair(ref, d):
        return ref[2 * d : 2 * d + 2].reshape(2 * ROWS, DIM)

    def row_block(d):
        have("p", d)
        s = TEMP * nt(both(q_chip), pair(p_all, d)) + pair_row(shf, d)
        s = jnp.where(keep_pair(d), s, NEG)
        s_ref[d] = s
        top = jnp.maximum(s[:, :ROWS], s[:, ROWS:])
        mx_ref[...] = top if d == 0 else jnp.maximum(mx_ref[...], top)

    def col_block(d):
        have("q", d)
        t = TEMP * nt(both(p_chip), pair(q_all, d)) + wide(sh_c)
        t_ref[d] = jnp.where(keep_pair(d), t, NEG)

    pl.when(z < 2)(lambda: side("p", 7, 6))
    pl.when(z >= 2)(lambda: side("p", 1, 2))
    second("p")
    y_first(1)
    y_first(3)
    calm = (z >= 2) & (z < 5)
    pl.when(calm)(lambda: z_first("q", 0, (1, -1, 2, -2)))
    pl.when(z < 2)(lambda: side("p", 1, 2))
    pl.when(z >= 2)(lambda: side("p", 7, 6))
    y_relay(0)
    y_first(2)
    cut_relay("p")
    pl.when(~calm)(lambda: z_first("q", 0, (1, -1, 2, -2)))
    x_first("q")
    x_send("q", 0)
    got("chip", q_chip)
    pl.when(z >= 6)(requests)
    row_block(0)
    x_pass("p", 3, 5, 4)
    row_block(1)
    row_block(7)
    second("q")
    y_relay(1)
    y_relay(3)
    row_block(2)
    row_block(6)
    side("q", 1, 2)
    side("q", 7, 6)
    y_relay(2)
    row_block(3)
    row_block(5)
    row_block(4)
    cut_relay("q")

    row_max = jnp.maximum(jnp.max(mx_ref[...], axis=1, keepdims=True), FLOOR)
    lane_sum = jnp.zeros((2 * ROWS, ROWS), F32)
    for d in range(NZ):
        e = jnp.exp(s_ref[d] - row_max)
        lane_sum = lane_sum + e[:, :ROWS] + e[:, ROWS:]
        e_ref[d] = e.astype(BF)
    row_sum = jnp.sum(lane_sum, axis=1, keepdims=True)
    max_a, sum_a = as_row(row_max[:ROWS]), as_row(row_sum[:ROWS])
    max_p, sum_p = as_row(row_max[ROWS:]), as_row(row_sum[ROWS:])
    stat_out[...] = jnp.where(iota((8, ROWS), 0) == 0, max_p, sum_p)
    send("stat", "stat", stat_out, stat_in, c_dev)

    x_pass("q", 3, 5, 4)
    got("bank", bank.at[pl.ds(0, 5 * NH)])

    q_own = q_chip[0]
    bank_max = None
    for k in range(BANK // ROWS):
        items = bank[4 * k : 4 * k + 4].reshape(ROWS, DIM)
        at = pl.ds(k, 1)
        shift = -bank_v[1, at, :].astype(F32) * UNIT
        keep = (bank_v[0, at, :].astype(F32) != id_c[:ROWS, :]) & (bank_v[2, at, :] < AGE_LIMIT)
        s = jnp.where(keep, TEMP * nt(q_own, items) + shift, NEG)
        sm_ref[k] = s
        bank_max = s if k == 0 else jnp.maximum(bank_max, s)
    max_m = jnp.maximum(jnp.max(bank_max, axis=1, keepdims=True), FLOOR)
    lane_sum = jnp.zeros((ROWS, ROWS), F32)
    for k in range(BANK // ROWS):
        e = jnp.exp(sm_ref[k] - max_m)
        lane_sum = lane_sum + e
        em_ref[:, k * ROWS : (k + 1) * ROWS] = e.astype(BF)
    max_c, sum_c = as_row(max_m), as_row(jnp.sum(lane_sum, axis=1, keepdims=True))

    got("stat", stat_in)
    max_b, sum_b = stat_in[0:1, :], stat_in[1:2, :]
    top = jnp.maximum(jnp.maximum(max_a, max_b), max_c)
    total = sum_a * jnp.exp(max_a - top) + sum_b * jnp.exp(max_b - top) + sum_c * jnp.exp(max_c - top)
    lse = top + jnp.log(total)
    lse_all[0] = jnp.broadcast_to(lse, (8, ROWS))
    for d in (4, 3, 5, 2, 6, 1, 7, 0):
        for col in (1, 0):
            if (col, d) != (0, 0):
                device = on_batch(xl if col == 0 else 1 - xl, lax.rem(z + d, NZ), core)
                send("lse", ("lse", d in (3, 4, 5)), lse_all.at[0], lse_all.at[2 * d + col], device)

    for d in range(NZ):
        part = nn(e_ref[d], pair(p_all, d))
        q_acc[...] = part if d == 0 else q_acc[...] + part
    half_out[...] = q_acc[ROWS:, :]
    send("half", "half", half_out, half_in, c_dev)
    mem_part = nn(em_ref[...], bank[...].reshape(BANK, DIM))

    for d in (0, 1, 7, 2, 6, 3, 5, 4):
        col_block(d)

    for d in (0, 1, 7, 2, 6, 3, 5, 4):
        if d == 0:
            got(("lse", False), lse_all.at[pl.ds(0, 9)])
        if d == 3:
            got(("lse", True), lse_all.at[pl.ds(0, 6)])
        level = jnp.concatenate([lse_all[2 * d][0:1, :], lse_all[2 * d + 1][0:1, :]], axis=1)
        coef = (jnp.exp(t_ref[d] - level) * pair_row(wf, d)).astype(BF)
        part = nn(coef, pair(q_all, d))
        p_acc[...] = part if d == 0 else p_acc[...] + part
    col_out[...] = p_acc[ROWS:, :]
    send("col", "col", col_out, col_in, c_dev)

    weight = wf[pl.ds(b, 1), :]
    scale = TEMP * weight
    fact_a = as_rows(scale * jnp.exp(max_a - lse))[:, 0:1]
    fact_b = as_rows(scale * jnp.exp(max_b - lse))[:, 0:1]
    fact_c = as_rows(scale * jnp.exp(max_c - lse))[:, 0:1]
    own_term = as_rows(scale)[:, 0:1]
    q_f, p_f = q_chip[0].astype(F32), p_chip[0].astype(F32)
    got("half", half_in)
    qgrad_out[...] = (
        fact_a * q_acc[:ROWS, :] + fact_b * half_in[...] + fact_c * mem_part - own_term * p_f
    )
    own_logit = TEMP * as_row(jnp.sum(q_f * p_f, axis=1, keepdims=True)) + shf[pl.ds(b, 1), :]
    loss_out[...] = lse - own_logit
    got("col", col_in)
    pgrad_out[...] = TEMP * (p_acc[:ROWS, :] + col_in[...]) - own_term * q_f

    assert (len(send_at), len(arrive_at)) == (SENDS, ARRIVALS)
    for out, ref in (
        ("p", blocks("p", 15)), ("q", blocks("q", 15)), ("bank", bank.at[pl.ds(0, 31)]),
        ("lse", lse_all.at[pl.ds(0, 15)]), ("chip", q_chip), ("stat", stat_out), ("half", half_out),
        ("col", col_out),
    ):
        sent(out, ref)


def hand_over(loss_in, qgrad_in, pgrad_in, loss_out, qgrad_out, pgrad_out):
    loss_out[...] = loss_in[...]
    qgrad_out[...] = qgrad_in[...]
    pgrad_out[...] = pgrad_in[...]


def body(queries, positives, pos_ids, pos_logq, mem_items, mem_ids, mem_logq, mem_age, counts):
    def lines(array):
        return array.reshape(-1, ROWS)

    any_spec = pl.BlockSpec(memory_space=pltpu.HBM)
    vmem_spec = pl.BlockSpec(memory_space=pltpu.VMEM)
    vmem = pltpu.VMEM
    scratch = [
        vmem((2 * NZ, ROWS, DIM), BF),
        vmem((2 * NZ, ROWS, DIM), BF),
        vmem((2, ROWS, DIM), BF),
        vmem((2, ROWS, DIM), BF),
        vmem((BLOCKS, SLOTS, DIM), BF),
        vmem((NZ, 2 * ROWS, 2 * ROWS), F32),
        vmem((NZ, 2 * ROWS, 2 * ROWS), F32),
        vmem((NZ, 2 * ROWS, 2 * ROWS), BF),
        vmem((2 * ROWS, ROWS), F32),
        vmem((ROWS, ROWS), jnp.int32),
        vmem((2, BLOCKS, ROWS), jnp.int32),
        vmem((3, 8, ROWS), jnp.int32),
        vmem((ROWS, ROWS), F32),
        vmem((ROWS, ROWS), F32),
        vmem((ROWS, ROWS), F32),
        vmem((BLOCKS, ROWS), F32),
        vmem((BLOCKS, ROWS), F32),
        vmem((BLOCKS, ROWS), F32),
        vmem((BLOCKS, ROWS), F32),
        vmem((2 * ROWS, ROWS), F32),
        vmem((2 * ROWS, ROWS), F32),
        vmem((2 * ROWS, ROWS), F32),
        vmem((8, ROWS), F32),
        vmem((8, ROWS), F32),
        vmem((2 * NZ, 8, ROWS), F32),
        vmem((ROWS, DIM), F32),
        vmem((ROWS, DIM), F32),
        vmem((ROWS, DIM), F32),
        vmem((ROWS, DIM), F32),
        vmem((2 * ROWS, DIM), F32),
        vmem((2 * ROWS, DIM), F32),
        vmem((BANK // ROWS, ROWS, ROWS), F32),
        vmem((ROWS, BANK), BF),
        pltpu.SemaphoreType.DMA((SENDS,)),
        pltpu.SemaphoreType.DMA((ARRIVALS,)),
        pltpu.SemaphoreType.DMA((LOADS,)),
    ]
    loss, query_grad, positive_grad = pl.pallas_call(
        kernel,
        out_shape=(
            jax.ShapeDtypeStruct((1, ROWS), F32),
            jax.ShapeDtypeStruct((ROWS, DIM), F32),
            jax.ShapeDtypeStruct((ROWS, DIM), F32),
        ),
        in_specs=[any_spec] * 9,
        out_specs=(vmem_spec, vmem_spec, vmem_spec),
        scratch_shapes=scratch,
        compiler_params=pltpu.CompilerParams(
            collective_id=0, has_side_effects=True, vmem_limit_bytes=67043328
        ),
        name="retrieval",
    )(
        queries, positives, mem_items, lines(counts), lines(pos_ids), lines(pos_logq),
        lines(mem_ids), lines(mem_logq), lines(mem_age),
    )
    loss, query_grad, positive_grad = pl.pallas_call(
        hand_over,
        out_shape=(
            jax.ShapeDtypeStruct((1, ROWS), F32),
            jax.ShapeDtypeStruct((ROWS, DIM), F32),
            jax.ShapeDtypeStruct((ROWS, DIM), F32),
        ),
        in_specs=[vmem_spec] * 3,
        out_specs=(vmem_spec, vmem_spec, vmem_spec),
        name="results",
    )(loss, query_grad, positive_grad)
    return loss.reshape(ROWS), query_grad, positive_grad


def solution(mesh):
    in_specs = (
        P(("mem", "batch"), None),
        P(("mem", "batch"), None),
        P(),
        P(),
        P(("batch", "mem"), None),
        P(),
        P(),
        P(),
        P(),
    )
    out_specs = (P(("mem", "batch")), P(("mem", "batch"), None), P(("mem", "batch"), None))
    return jax.shard_map(body, mesh=mesh, in_specs=in_specs, out_specs=out_specs, check_vma=False)
```

```python
import jax
import jax.numpy as jnp
from jax import lax
from jax.experimental import pallas as pl
from jax.experimental.pallas import tpu as pltpu
from jax.sharding import PartitionSpec as P

MESH = pl.DeviceIdType.MESH
AGE_LIMIT = 16
NZ, NY, NH = 8, 8, 4
ROWS, DIM, CUT = 128, 256, 32
BLOCKS = 32
GROUP = ROWS * BLOCKS
SLOTS = 32
BANK = 1024
WINDOW = 34
TEMP = 8.0
UNIT = 1.0 / 1024.0
NEG = -1e30
FLOOR = -1e20
SENDS, ARRIVALS, LOADS = 8, 42, 5
BF, F32 = jnp.bfloat16, jnp.float32


def nt(left, right):
    return lax.dot_general(left, right, (((1,), (1,)), ((), ())), preferred_element_type=F32)


def nn(left, right):
    return lax.dot_general(left, right, (((1,), (0,)), ((), ())), preferred_element_type=F32)


def iota(shape, dim):
    return lax.broadcasted_iota(jnp.int32, shape, dim)


def as_rows(row):
    return jnp.broadcast_to(row, (ROWS, ROWS)).T


def as_row(column):
    return jnp.broadcast_to(column, (ROWS, ROWS)).T[0:1, :]


def kernel(
    q_hbm, p_hbm, items_hbm, counts_hbm, ids_hbm, logq_hbm, bids_hbm, blogq_hbm, bage_hbm,
    loss_out, qgrad_out, pgrad_out,
    q_all, p_all, q_chip, p_chip, bank,
    s_ref, t_ref, e_ref, mx_ref,
    counts_v, lines_v, bank_v,
    hi_ref, lo_ref, dd_ref, idf, reqf, shf, wf, id_c, req_c, sh_c,
    stat_out, stat_in, lse_all, half_out, half_in, col_out, col_in, q_acc, p_acc,
    sm_ref, em_ref,
    send_sems, recv_sems, local_sems,
):
    b = lax.axis_index("batch")
    m = lax.axis_index("mem")
    core = lax.rem(b, 2)
    z = lax.rem(lax.div(b, 2), NZ)
    xl = lax.div(b, 2 * NZ)
    y = lax.rem(m, NY)
    xh = lax.div(m, NY)

    def on_batch(x_at, z_at, core_at):
        return {"batch": x_at * (2 * NZ) + z_at * 2 + core_at, "mem": m}

    def on_mem(h_at, y_at):
        return {"batch": b, "mem": h_at * NY + y_at}

    def z_dev(hop):
        return on_batch(xl, lax.rem(z + hop + NZ, NZ), core)

    def y_dev(hop):
        return on_mem(xh, lax.rem(y + hop + NY, NY))

    x_dev = on_batch(1 - xl, z, core)
    c_dev = on_batch(xl, z, 1 - core)
    h_dev = {e: on_mem(lax.rem(xh + e, NH), y) for e in (1, 3)}

    send_at, arrive_at = {}, {}

    def send(out, into, src, dst, device):
        pltpu.make_async_remote_copy(
            src_ref=src,
            dst_ref=dst,
            send_sem=send_sems.at[send_at.setdefault(out, len(send_at))],
            recv_sem=recv_sems.at[arrive_at.setdefault(into, len(arrive_at))],
            device_id=device,
            device_id_type=MESH,
        ).start()

    def waiting(sem, ref):
        pltpu.make_async_copy(ref, ref, sem).wait()

    def sent(out, ref):
        waiting(send_sems.at[send_at[out]], ref)

    def got(into, ref):
        waiting(recv_sems.at[arrive_at[into]], ref)

    def load(kind, src, dst):
        pltpu.make_async_copy(src, dst, local_sems.at[kind]).start()

    load(0, counts_hbm, counts_v)
    load(1, ids_hbm.at[pl.ds(m * BLOCKS, BLOCKS)], lines_v.at[0])
    load(1, logq_hbm.at[pl.ds(m * BLOCKS, BLOCKS)], lines_v.at[1])
    load(2, bids_hbm.at[pl.ds(b * 8, 8)], bank_v.at[0])
    load(2, blogq_hbm.at[pl.ds(b * 8, 8)], bank_v.at[1])
    load(2, bage_hbm.at[pl.ds(b * 8, 8)], bank_v.at[2])
    load(3, q_hbm, q_all.at[0])
    load(3, p_hbm, p_all.at[0])
    load(3, q_hbm, q_chip.at[0])
    load(3, p_hbm, p_chip.at[0])
    load(4, items_hbm, bank.at[m])

    def requests():
        waiting(local_sems.at[0], counts_v)
        waiting(local_sems.at[1], lines_v)
        sub, lane = iota((ROWS, ROWS), 0), iota((ROWS, ROWS), 1)
        upper = (sub <= lane).astype(F32).astype(BF)
        lower = (lane < sub).astype(F32).astype(BF)
        count = counts_v[...].astype(F32)
        count_bf = count.astype(BF)
        ends = nn(count_bf, upper) + jnp.sum(nn(lower, count_bf), axis=1, keepdims=True)
        ends = ends - (m * GROUP).astype(F32)
        starts = ends - count
        inside = (ends > 0.0) & (starts < float(GROUP))
        before = pltpu.roll(count, 1, 1)
        before = jnp.where(lane == 0, pltpu.roll(before, 1, 0), before)
        dd_ref[...] = jnp.where(starts <= 0.0, count, count - before)
        starts = jnp.maximum(starts, 0.0)
        high = jnp.floor(starts * (1.0 / ROWS))
        lo_ref[...] = starts - high * ROWS
        hi_ref[...] = jnp.where(inside, high, 999.0)
        passed = jnp.sum((ends[:, ROWS - 1 :] <= 0.0).astype(F32))
        first = jnp.minimum(passed.astype(jnp.int32), ROWS - WINDOW)
        sub32 = iota((BLOCKS, ROWS), 0).astype(F32)
        subf = sub.astype(F32)

        def scatter(step, total):
            lefts, rights = [], []
            for k in range(2):
                at = pl.ds(first + 2 * step + k, 1)
                same = hi_ref[at, :] == sub32
                mark = jnp.where(same, 1.0, 0.0)
                delta = jnp.where(same, dd_ref[at, :], 0.0)
                lefts.append(jnp.concatenate([mark, delta], axis=0).astype(BF))
                rights.append(jnp.where(lo_ref[at, :] == subf, 1.0, 0.0).astype(BF))
            return total + nt(jnp.concatenate(lefts, axis=1), jnp.concatenate(rights, axis=1))

        marks = lax.fori_loop(0, WINDOW // 2, scatter, jnp.zeros((2 * BLOCKS, ROWS), F32))
        low32 = (iota((BLOCKS, BLOCKS), 1) < iota((BLOCKS, BLOCKS), 0)).astype(F32).astype(BF)

        def running(part):
            part = part.astype(BF)
            return nn(part, upper) + jnp.sum(nn(low32, part), axis=1, keepdims=True)

        reqf[...] = running(marks[:BLOCKS])
        wf[...] = 1.0 / running(marks[BLOCKS:])
        idf[...] = lines_v[0].astype(F32)
        shf[...] = -lines_v[1].astype(F32) * UNIT
        chip_rows = (b, b + 1 - 2 * core)
        for k, at in enumerate(chip_rows):
            rows = pl.ds(k * ROWS, ROWS)
            id_c[rows, :] = as_rows(idf[pl.ds(at, 1), :])
            req_c[rows, :] = as_rows(reqf[pl.ds(at, 1), :])
            sh_c[rows, :] = as_rows(shf[pl.ds(at, 1), :])

    barrier = pltpu.get_barrier_semaphore()
    near = [place(hop) for place in (z_dev, y_dev) for hop in (1, -1, 2, -2)]
    near += [x_dev, c_dev, h_dev[1], h_dev[3]]
    for device in near:
        pl.semaphore_signal(barrier, inc=1, device_id=device, device_id_type=MESH)
    pl.when(z < 6)(requests)
    pl.semaphore_wait(barrier, len(near))

    own = {"q": q_hbm, "p": p_hbm}
    held = {"q": q_all, "p": p_all}
    onward = {"p": ((2, 1), (2, 2), (6, -1)), "q": ((2, 1), (6, -1), (6, -2))}

    def blocks(arr, n):
        return held[arr].at[pl.ds(0, n)]

    def piece(arr, col, d):
        if col == 0 and d == 0:
            return own[arr]
        return held[arr].at[2 * d] if col == 0 else held[arr].at[2 * d + 1, pl.ds(0, CUT)]

    final = {1: "near", 7: "near", 3: "far", 5: "far", 4: "last"}

    def z_send(arr, col, d, hop):
        there = (d + hop) % NZ
        block = held[arr].at[2 * there + col]
        dst = block if col == 0 else held[arr].at[2 * there + 1, pl.ds(0, CUT)]
        into = there if col == 0 else final.get(there, "cut")
        send(arr, (arr, into), piece(arr, col, d), dst, z_dev(hop))

    def z_first(arr, col, hops):
        for hop in hops:
            z_send(arr, col, 0, hop)

    def side(arr, near, far):
        got((arr, near), blocks(arr, 1))
        x_send(arr, near)
        got((arr, far), blocks(arr, 1))
        for d, hop in onward[arr]:
            if d == far:
                z_send(arr, 0, d, hop)
        x_send(arr, far)

    def cut_relay(arr):
        got((arr, "cut"), held[arr].at[1, pl.ds(0, 2 * CUT)])
        for d, hop in onward[arr]:
            z_send(arr, 1, d, hop)

    def x_first(arr):
        src, dst = own[arr].at[pl.ds(0, CUT)], held[arr].at[1, pl.ds(0, CUT)]
        send(arr, (arr, "first"), src, dst, x_dev)

    def x_send(arr, d):
        rest = pl.ds(CUT, ROWS - CUT)
        src = own[arr].at[rest] if d == 0 else held[arr].at[2 * d, rest]
        into = final.get(d, "x0" if d == 0 else "x2")
        send(arr, (arr, into), src, held[arr].at[2 * d + 1, rest], x_dev)

    def x_pass(arr, *group):
        for d in group:
            got((arr, d), blocks(arr, 1))
            x_send(arr, d)

    def second(arr):
        got((arr, "first"), held[arr].at[1, pl.ds(0, CUT)])
        z_first(arr, 1, (1, -1, 2, -2))

    def have(arr, d):
        rest = ROWS - CUT
        if d == 0:
            got((arr, "x0"), held[arr].at[1, pl.ds(0, rest)])
        if d == 2:
            got((arr, "x2"), held[arr].at[pl.ds(0, 2), pl.ds(0, rest)])
        if d in (1, 3):
            got((arr, final[d]), blocks(arr, 2))
        if d == 4:
            got((arr, final[d]), blocks(arr, 1))

    def bank_at(e, dy):
        return lax.rem(xh + NH - e, NH) * NY + lax.rem(y + NY - dy, NY)

    def y_send(e, d, hop):
        at, there = bank_at(e, d), (d + hop) % NY
        src = items_hbm if (e, d) == (0, 0) else bank.at[at]
        into = ("bank", e) if there in (2, 6) else "bank"
        send("bank", into, src, bank.at[at], y_dev(hop))

    def y_first(e):
        if e:
            got(("h", e), bank.at[0])
        if e == 1:
            send("bank", ("h", 2), bank.at[bank_at(1, 0)], bank.at[bank_at(1, 0)], h_dev[1])
        for hop in (1, -1, 2, -2):
            y_send(e, 0, hop)

    def y_relay(e):
        got(("bank", e), bank.at[pl.ds(0, 2)])
        for d, hop in ((2, 1), (2, 2), (6, -1)) if e in (0, 1) else ((2, 1), (6, -1), (6, -2)):
            y_send(e, d, hop)

    z_first("p", 0, (2, -2, 1, -1))
    x_first("p")
    for e in (1, 3):
        send("bank", ("h", e), items_hbm, bank.at[m], h_dev[e])
    y_first(0)
    x_send("p", 0)
    send("chip", "chip", q_hbm, q_chip.at[1], c_dev)
    send("chip", "chip", p_hbm, p_chip.at[1], c_dev)
    waiting(local_sems.at[2], bank_v)
    waiting(local_sems.at[3], blocks("q", 4))
    waiting(local_sems.at[4], bank.at[0])

    def pair_row(ref, d):
        z_at = lax.rem(z + NZ - d, NZ)
        parts = [ref[pl.ds(x_at * (2 * NZ) + z_at * 2 + core, 1), :] for x_at in (xl, 1 - xl)]
        return jnp.concatenate(parts, axis=1)

    def wide(ref):
        part = ref[...]
        return jnp.concatenate([part, part], axis=1)

    def keep_pair(d):
        keep = (wide(id_c) != pair_row(idf, d)) & (wide(req_c) != pair_row(reqf, d))
        if d == 0:
            keep = keep | (iota((2 * ROWS, 2 * ROWS), 0) == iota((2 * ROWS, 2 * ROWS), 1)) & (
                iota((2 * ROWS, 2 * ROWS), 0) < ROWS
            )
        return keep

    def both(ref):
        return ref[...].reshape(2 * ROWS, DIM)

    def pair(ref, d):
        return ref[2 * d : 2 * d + 2].reshape(2 * ROWS, DIM)

    def row_block(d):
        have("p", d)
        s = TEMP * nt(both(q_chip), pair(p_all, d)) + pair_row(shf, d)
        s = jnp.where(keep_pair(d), s, NEG)
        s_ref[d] = s
        top = jnp.maximum(s[:, :ROWS], s[:, ROWS:])
        mx_ref[...] = top if d == 0 else jnp.maximum(mx_ref[...], top)

    def col_block(d):
        have("q", d)
        t = TEMP * nt(both(p_chip), pair(q_all, d)) + wide(sh_c)
        t_ref[d] = jnp.where(keep_pair(d), t, NEG)

    pl.when(z < 2)(lambda: side("p", 7, 6))
    pl.when(z >= 2)(lambda: side("p", 1, 2))
    second("p")
    y_first(1)
    y_first(3)
    calm = (z >= 2) & (z < 5)
    pl.when(calm)(lambda: z_first("q", 0, (1, -1, 2, -2)))
    pl.when(z < 2)(lambda: side("p", 1, 2))
    pl.when(z >= 2)(lambda: side("p", 7, 6))
    y_relay(0)
    y_first(2)
    cut_relay("p")
    pl.when(~calm)(lambda: z_first("q", 0, (1, -1, 2, -2)))
    x_first("q")
    x_send("q", 0)
    got("chip", q_chip)
    pl.when(z >= 6)(requests)
    row_block(0)
    second("q")
    x_pass("p", 3, 5, 4)
    row_block(1)
    row_block(7)
    y_relay(1)
    y_relay(3)
    row_block(2)
    row_block(6)
    side("q", 1, 2)
    side("q", 7, 6)
    y_relay(2)
    row_block(3)
    row_block(5)
    got("bank", bank.at[pl.ds(0, 5 * NH)])
    q_own = q_chip[0]
    bank_max = None
    for k in range(BANK // ROWS):
        items = bank[4 * k : 4 * k + 4].reshape(ROWS, DIM)
        at = pl.ds(k, 1)
        shift = -bank_v[1, at, :].astype(F32) * UNIT
        keep = (bank_v[0, at, :].astype(F32) != id_c[:ROWS, :]) & (bank_v[2, at, :] < AGE_LIMIT)
        s = jnp.where(keep, TEMP * nt(q_own, items) + shift, NEG)
        sm_ref[k] = s
        bank_max = s if k == 0 else jnp.maximum(bank_max, s)
    max_m = jnp.maximum(jnp.max(bank_max, axis=1, keepdims=True), FLOOR)
    lane_sum = jnp.zeros((ROWS, ROWS), F32)
    for k in range(BANK // ROWS):
        e = jnp.exp(sm_ref[k] - max_m)
        lane_sum = lane_sum + e
        em_ref[:, k * ROWS : (k + 1) * ROWS] = e.astype(BF)
    max_c, sum_c = as_row(max_m), as_row(jnp.sum(lane_sum, axis=1, keepdims=True))

    row_block(4)

    row_max = jnp.maximum(jnp.max(mx_ref[...], axis=1, keepdims=True), FLOOR)
    lane_sum = jnp.zeros((2 * ROWS, ROWS), F32)
    for d in range(NZ):
        e = jnp.exp(s_ref[d] - row_max)
        lane_sum = lane_sum + e[:, :ROWS] + e[:, ROWS:]
        e_ref[d] = e.astype(BF)
    row_sum = jnp.sum(lane_sum, axis=1, keepdims=True)
    max_a, sum_a = as_row(row_max[:ROWS]), as_row(row_sum[:ROWS])
    max_p, sum_p = as_row(row_max[ROWS:]), as_row(row_sum[ROWS:])
    stat_out[...] = jnp.where(iota((8, ROWS), 0) == 0, max_p, sum_p)
    send("stat", "stat", stat_out, stat_in, c_dev)

    got("stat", stat_in)
    max_b, sum_b = stat_in[0:1, :], stat_in[1:2, :]
    top = jnp.maximum(jnp.maximum(max_a, max_b), max_c)
    total = sum_a * jnp.exp(max_a - top) + sum_b * jnp.exp(max_b - top) + sum_c * jnp.exp(max_c - top)
    lse = top + jnp.log(total)
    lse_all[0] = jnp.broadcast_to(lse, (8, ROWS))
    for d in (4, 3, 5, 2, 6, 1, 7, 0):
        for col in (1, 0):
            if (col, d) != (0, 0):
                device = on_batch(xl if col == 0 else 1 - xl, lax.rem(z + d, NZ), core)
                send("lse", ("lse", d in (3, 4, 5)), lse_all.at[0], lse_all.at[2 * d + col], device)

    cut_relay("q")
    x_pass("q", 3, 5, 4)
    for d in range(NZ):
        part = nn(e_ref[d], pair(p_all, d))
        q_acc[...] = part if d == 0 else q_acc[...] + part
    half_out[...] = q_acc[ROWS:, :]
    send("half", "half", half_out, half_in, c_dev)
    mem_part = nn(em_ref[...], bank[...].reshape(BANK, DIM))

    for d in (0, 1, 7, 2, 6, 3, 5, 4):
        col_block(d)

    for d in (0, 1, 7, 2, 6, 3, 5, 4):
        if d == 0:
            got(("lse", False), lse_all.at[pl.ds(0, 9)])
        if d == 3:
            got(("lse", True), lse_all.at[pl.ds(0, 6)])
        level = jnp.concatenate([lse_all[2 * d][0:1, :], lse_all[2 * d + 1][0:1, :]], axis=1)
        coef = (jnp.exp(t_ref[d] - level) * pair_row(wf, d)).astype(BF)
        part = nn(coef, pair(q_all, d))
        p_acc[...] = part if d == 0 else p_acc[...] + part
    col_out[...] = p_acc[ROWS:, :]
    send("col", "col", col_out, col_in, c_dev)

    weight = wf[pl.ds(b, 1), :]
    scale = TEMP * weight
    fact_a = as_rows(scale * jnp.exp(max_a - lse))[:, 0:1]
    fact_b = as_rows(scale * jnp.exp(max_b - lse))[:, 0:1]
    fact_c = as_rows(scale * jnp.exp(max_c - lse))[:, 0:1]
    own_term = as_rows(scale)[:, 0:1]
    q_f, p_f = q_chip[0].astype(F32), p_chip[0].astype(F32)
    got("half", half_in)
    qgrad_out[...] = (
        fact_a * q_acc[:ROWS, :] + fact_b * half_in[...] + fact_c * mem_part - own_term * p_f
    )
    own_logit = TEMP * as_row(jnp.sum(q_f * p_f, axis=1, keepdims=True)) + shf[pl.ds(b, 1), :]
    loss_out[...] = lse - own_logit
    got("col", col_in)
    pgrad_out[...] = TEMP * (p_acc[:ROWS, :] + col_in[...]) - own_term * q_f

    assert (len(send_at), len(arrive_at)) == (SENDS, ARRIVALS)
    for out, ref in (
        ("p", blocks("p", 15)), ("q", blocks("q", 15)), ("bank", bank.at[pl.ds(0, 31)]),
        ("lse", lse_all.at[pl.ds(0, 15)]), ("chip", q_chip), ("stat", stat_out), ("half", half_out),
        ("col", col_out),
    ):
        sent(out, ref)


def hand_over(loss_in, qgrad_in, pgrad_in, loss_out, qgrad_out, pgrad_out):
    loss_out[...] = loss_in[...]
    qgrad_out[...] = qgrad_in[...]
    pgrad_out[...] = pgrad_in[...]


def body(queries, positives, pos_ids, pos_logq, mem_items, mem_ids, mem_logq, mem_age, counts):
    def lines(array):
        return array.reshape(-1, ROWS)

    any_spec = pl.BlockSpec(memory_space=pltpu.HBM)
    vmem_spec = pl.BlockSpec(memory_space=pltpu.VMEM)
    vmem = pltpu.VMEM
    scratch = [
        vmem((2 * NZ, ROWS, DIM), BF),
        vmem((2 * NZ, ROWS, DIM), BF),
        vmem((2, ROWS, DIM), BF),
        vmem((2, ROWS, DIM), BF),
        vmem((BLOCKS, SLOTS, DIM), BF),
        vmem((NZ, 2 * ROWS, 2 * ROWS), F32),
        vmem((NZ, 2 * ROWS, 2 * ROWS), F32),
        vmem((NZ, 2 * ROWS, 2 * ROWS), BF),
        vmem((2 * ROWS, ROWS), F32),
        vmem((ROWS, ROWS), jnp.int32),
        vmem((2, BLOCKS, ROWS), jnp.int32),
        vmem((3, 8, ROWS), jnp.int32),
        vmem((ROWS, ROWS), F32),
        vmem((ROWS, ROWS), F32),
        vmem((ROWS, ROWS), F32),
        vmem((BLOCKS, ROWS), F32),
        vmem((BLOCKS, ROWS), F32),
        vmem((BLOCKS, ROWS), F32),
        vmem((BLOCKS, ROWS), F32),
        vmem((2 * ROWS, ROWS), F32),
        vmem((2 * ROWS, ROWS), F32),
        vmem((2 * ROWS, ROWS), F32),
        vmem((8, ROWS), F32),
        vmem((8, ROWS), F32),
        vmem((2 * NZ, 8, ROWS), F32),
        vmem((ROWS, DIM), F32),
        vmem((ROWS, DIM), F32),
        vmem((ROWS, DIM), F32),
        vmem((ROWS, DIM), F32),
        vmem((2 * ROWS, DIM), F32),
        vmem((2 * ROWS, DIM), F32),
        vmem((BANK // ROWS, ROWS, ROWS), F32),
        vmem((ROWS, BANK), BF),
        pltpu.SemaphoreType.DMA((SENDS,)),
        pltpu.SemaphoreType.DMA((ARRIVALS,)),
        pltpu.SemaphoreType.DMA((LOADS,)),
    ]
    loss, query_grad, positive_grad = pl.pallas_call(
        kernel,
        out_shape=(
            jax.ShapeDtypeStruct((1, ROWS), F32),
            jax.ShapeDtypeStruct((ROWS, DIM), F32),
            jax.ShapeDtypeStruct((ROWS, DIM), F32),
        ),
        in_specs=[any_spec] * 9,
        out_specs=(vmem_spec, vmem_spec, vmem_spec),
        scratch_shapes=scratch,
        compiler_params=pltpu.CompilerParams(
            collective_id=0, has_side_effects=True, vmem_limit_bytes=67043328
        ),
        name="retrieval",
    )(
        queries, positives, mem_items, lines(counts), lines(pos_ids), lines(pos_logq),
        lines(mem_ids), lines(mem_logq), lines(mem_age),
    )
    loss, query_grad, positive_grad = pl.pallas_call(
        hand_over,
        out_shape=(
            jax.ShapeDtypeStruct((1, ROWS), F32),
            jax.ShapeDtypeStruct((ROWS, DIM), F32),
            jax.ShapeDtypeStruct((ROWS, DIM), F32),
        ),
        in_specs=[vmem_spec] * 3,
        out_specs=(vmem_spec, vmem_spec, vmem_spec),
        name="results",
    )(loss, query_grad, positive_grad)
    return loss.reshape(ROWS), query_grad, positive_grad


def solution(mesh):
    in_specs = (
        P(("mem", "batch"), None),
        P(("mem", "batch"), None),
        P(),
        P(),
        P(("batch", "mem"), None),
        P(),
        P(),
        P(),
        P(),
    )
    out_specs = (P(("mem", "batch")), P(("mem", "batch"), None), P(("mem", "batch"), None))
    return jax.shard_map(body, mesh=mesh, in_specs=in_specs, out_specs=out_specs, check_vma=False)
```

```python
import jax
import jax.numpy as jnp
from jax import lax
from jax.experimental import pallas as pl
from jax.experimental.pallas import tpu as pltpu
from jax.sharding import PartitionSpec as P

MESH = pl.DeviceIdType.MESH
AGE_LIMIT = 16
NZ, NY, NH = 8, 8, 4
ROWS, DIM, CUT = 128, 256, 32
BLOCKS = 32
GROUP = ROWS * BLOCKS
SLOTS = 32
BANK = 1024
WINDOW = 34
TEMP = 8.0
UNIT = 1.0 / 1024.0
NEG = -1e30
FLOOR = -1e20
SENDS, ARRIVALS, LOADS = 8, 42, 5
BF, F32 = jnp.bfloat16, jnp.float32


def nt(left, right):
    return lax.dot_general(left, right, (((1,), (1,)), ((), ())), preferred_element_type=F32)


def nn(left, right):
    return lax.dot_general(left, right, (((1,), (0,)), ((), ())), preferred_element_type=F32)


def iota(shape, dim):
    return lax.broadcasted_iota(jnp.int32, shape, dim)


def as_rows(row):
    return jnp.broadcast_to(row, (ROWS, ROWS)).T


def as_row(column):
    return jnp.broadcast_to(column, (ROWS, ROWS)).T[0:1, :]


def kernel(
    q_hbm, p_hbm, items_hbm, counts_hbm, ids_hbm, logq_hbm, bids_hbm, blogq_hbm, bage_hbm,
    loss_out, qgrad_out, pgrad_out,
    q_all, p_all, q_chip, p_chip, bank,
    s_ref, t_ref, e_ref, mx_ref,
    counts_v, lines_v, bank_v,
    hi_ref, lo_ref, dd_ref, idf, reqf, shf, wf, id_c, req_c, sh_c,
    stat_out, stat_in, lse_all, half_out, half_in, col_out, col_in, q_acc, p_acc,
    sm_ref, em_ref,
    send_sems, recv_sems, local_sems,
):
    b = lax.axis_index("batch")
    m = lax.axis_index("mem")
    core = lax.rem(b, 2)
    z = lax.rem(lax.div(b, 2), NZ)
    xl = lax.div(b, 2 * NZ)
    y = lax.rem(m, NY)
    xh = lax.div(m, NY)

    def on_batch(x_at, z_at, core_at):
        return {"batch": x_at * (2 * NZ) + z_at * 2 + core_at, "mem": m}

    def on_mem(h_at, y_at):
        return {"batch": b, "mem": h_at * NY + y_at}

    def z_dev(hop):
        return on_batch(xl, lax.rem(z + hop + NZ, NZ), core)

    def y_dev(hop):
        return on_mem(xh, lax.rem(y + hop + NY, NY))

    x_dev = on_batch(1 - xl, z, core)
    c_dev = on_batch(xl, z, 1 - core)
    h_dev = {e: on_mem(lax.rem(xh + e, NH), y) for e in (1, 3)}

    send_at, arrive_at = {}, {}

    def send(out, into, src, dst, device):
        pltpu.make_async_remote_copy(
            src_ref=src,
            dst_ref=dst,
            send_sem=send_sems.at[send_at.setdefault(out, len(send_at))],
            recv_sem=recv_sems.at[arrive_at.setdefault(into, len(arrive_at))],
            device_id=device,
            device_id_type=MESH,
        ).start()

    def waiting(sem, ref):
        pltpu.make_async_copy(ref, ref, sem).wait()

    def sent(out, ref):
        waiting(send_sems.at[send_at[out]], ref)

    def got(into, ref):
        waiting(recv_sems.at[arrive_at[into]], ref)

    def load(kind, src, dst):
        pltpu.make_async_copy(src, dst, local_sems.at[kind]).start()

    load(0, counts_hbm, counts_v)
    load(1, ids_hbm.at[pl.ds(m * BLOCKS, BLOCKS)], lines_v.at[0])
    load(1, logq_hbm.at[pl.ds(m * BLOCKS, BLOCKS)], lines_v.at[1])
    load(2, bids_hbm.at[pl.ds(b * 8, 8)], bank_v.at[0])
    load(2, blogq_hbm.at[pl.ds(b * 8, 8)], bank_v.at[1])
    load(2, bage_hbm.at[pl.ds(b * 8, 8)], bank_v.at[2])
    load(3, q_hbm, q_all.at[0])
    load(3, p_hbm, p_all.at[0])
    load(3, q_hbm, q_chip.at[0])
    load(3, p_hbm, p_chip.at[0])
    load(4, items_hbm, bank.at[m])

    def requests():
        waiting(local_sems.at[0], counts_v)
        waiting(local_sems.at[1], lines_v)
        sub, lane = iota((ROWS, ROWS), 0), iota((ROWS, ROWS), 1)
        upper = (sub <= lane).astype(F32).astype(BF)
        lower = (lane < sub).astype(F32).astype(BF)
        count = counts_v[...].astype(F32)
        count_bf = count.astype(BF)
        ends = nn(count_bf, upper) + jnp.sum(nn(lower, count_bf), axis=1, keepdims=True)
        ends = ends - (m * GROUP).astype(F32)
        starts = ends - count
        inside = (ends > 0.0) & (starts < float(GROUP))
        before = pltpu.roll(count, 1, 1)
        before = jnp.where(lane == 0, pltpu.roll(before, 1, 0), before)
        dd_ref[...] = jnp.where(starts <= 0.0, count, count - before)
        starts = jnp.maximum(starts, 0.0)
        high = jnp.floor(starts * (1.0 / ROWS))
        lo_ref[...] = starts - high * ROWS
        hi_ref[...] = jnp.where(inside, high, 999.0)
        passed = jnp.sum((ends[:, ROWS - 1 :] <= 0.0).astype(F32))
        first = jnp.minimum(passed.astype(jnp.int32), ROWS - WINDOW)
        sub32 = iota((BLOCKS, ROWS), 0).astype(F32)
        subf = sub.astype(F32)

        def scatter(step, total):
            lefts, rights = [], []
            for k in range(2):
                at = pl.ds(first + 2 * step + k, 1)
                same = hi_ref[at, :] == sub32
                mark = jnp.where(same, 1.0, 0.0)
                delta = jnp.where(same, dd_ref[at, :], 0.0)
                lefts.append(jnp.concatenate([mark, delta], axis=0).astype(BF))
                rights.append(jnp.where(lo_ref[at, :] == subf, 1.0, 0.0).astype(BF))
            return total + nt(jnp.concatenate(lefts, axis=1), jnp.concatenate(rights, axis=1))

        marks = lax.fori_loop(0, WINDOW // 2, scatter, jnp.zeros((2 * BLOCKS, ROWS), F32))
        low32 = (iota((BLOCKS, BLOCKS), 1) < iota((BLOCKS, BLOCKS), 0)).astype(F32).astype(BF)

        def running(part):
            part = part.astype(BF)
            return nn(part, upper) + jnp.sum(nn(low32, part), axis=1, keepdims=True)

        reqf[...] = running(marks[:BLOCKS])
        wf[...] = 1.0 / running(marks[BLOCKS:])
        idf[...] = lines_v[0].astype(F32)
        shf[...] = -lines_v[1].astype(F32) * UNIT
        chip_rows = (b, b + 1 - 2 * core)
        for k, at in enumerate(chip_rows):
            rows = pl.ds(k * ROWS, ROWS)
            id_c[rows, :] = as_rows(idf[pl.ds(at, 1), :])
            req_c[rows, :] = as_rows(reqf[pl.ds(at, 1), :])
            sh_c[rows, :] = as_rows(shf[pl.ds(at, 1), :])

    barrier = pltpu.get_barrier_semaphore()
    near = [place(hop) for place in (z_dev, y_dev) for hop in (1, -1, 2, -2)]
    near += [x_dev, c_dev, h_dev[1], h_dev[3]]
    for device in near:
        pl.semaphore_signal(barrier, inc=1, device_id=device, device_id_type=MESH)
    pl.when(z < 6)(requests)
    pl.semaphore_wait(barrier, len(near))

    own = {"q": q_hbm, "p": p_hbm}
    held = {"q": q_all, "p": p_all}
    onward = {"p": ((2, 1), (2, 2), (6, -1)), "q": ((2, 1), (6, -1), (6, -2))}

    def blocks(arr, n):
        return held[arr].at[pl.ds(0, n)]

    def piece(arr, col, d):
        if col == 0 and d == 0:
            return own[arr]
        return held[arr].at[2 * d] if col == 0 else held[arr].at[2 * d + 1, pl.ds(0, CUT)]

    final = {1: "near", 7: "near", 3: "far", 5: "far", 4: "last"}

    def z_send(arr, col, d, hop):
        there = (d + hop) % NZ
        block = held[arr].at[2 * there + col]
        dst = block if col == 0 else held[arr].at[2 * there + 1, pl.ds(0, CUT)]
        into = there if col == 0 else final.get(there, "cut")
        send(arr, (arr, into), piece(arr, col, d), dst, z_dev(hop))

    def z_first(arr, col, hops):
        for hop in hops:
            z_send(arr, col, 0, hop)

    def side(arr, near, far):
        got((arr, near), blocks(arr, 1))
        x_send(arr, near)
        got((arr, far), blocks(arr, 1))
        for d, hop in onward[arr]:
            if d == far:
                z_send(arr, 0, d, hop)
        x_send(arr, far)

    def cut_relay(arr):
        got((arr, "cut"), held[arr].at[1, pl.ds(0, 2 * CUT)])
        for d, hop in onward[arr]:
            z_send(arr, 1, d, hop)

    def x_first(arr):
        src, dst = own[arr].at[pl.ds(0, CUT)], held[arr].at[1, pl.ds(0, CUT)]
        send(arr, (arr, "first"), src, dst, x_dev)

    def x_send(arr, d):
        rest = pl.ds(CUT, ROWS - CUT)
        src = own[arr].at[rest] if d == 0 else held[arr].at[2 * d, rest]
        into = final.get(d, "x0" if d == 0 else "x2")
        send(arr, (arr, into), src, held[arr].at[2 * d + 1, rest], x_dev)

    def x_pass(arr, *group):
        for d in group:
            got((arr, d), blocks(arr, 1))
            x_send(arr, d)

    def second(arr):
        got((arr, "first"), held[arr].at[1, pl.ds(0, CUT)])
        z_first(arr, 1, (1, -1, 2, -2))

    def have(arr, d):
        rest = ROWS - CUT
        if d == 0:
            got((arr, "x0"), held[arr].at[1, pl.ds(0, rest)])
        if d == 2:
            got((arr, "x2"), held[arr].at[pl.ds(0, 2), pl.ds(0, rest)])
        if d in (1, 3):
            got((arr, final[d]), blocks(arr, 2))
        if d == 4:
            got((arr, final[d]), blocks(arr, 1))

    def bank_at(e, dy):
        return lax.rem(xh + NH - e, NH) * NY + lax.rem(y + NY - dy, NY)

    def y_send(e, d, hop):
        at, there = bank_at(e, d), (d + hop) % NY
        src = items_hbm if (e, d) == (0, 0) else bank.at[at]
        into = ("bank", e) if there in (2, 6) else "bank"
        send("bank", into, src, bank.at[at], y_dev(hop))

    def y_first(e):
        if e:
            got(("h", e), bank.at[0])
        if e == 1:
            send("bank", ("h", 2), bank.at[bank_at(1, 0)], bank.at[bank_at(1, 0)], h_dev[1])
        for hop in (1, -1, 2, -2):
            y_send(e, 0, hop)

    def y_relay(e):
        got(("bank", e), bank.at[pl.ds(0, 2)])
        for d, hop in ((2, 1), (2, 2), (6, -1)) if e in (0, 1) else ((2, 1), (6, -1), (6, -2)):
            y_send(e, d, hop)

    z_first("p", 0, (2, -2, 1, -1))
    x_first("p")
    for e in (1, 3):
        send("bank", ("h", e), items_hbm, bank.at[m], h_dev[e])
    y_first(0)
    x_send("p", 0)
    send("chip", "chip", q_hbm, q_chip.at[1], c_dev)
    send("chip", "chip", p_hbm, p_chip.at[1], c_dev)
    waiting(local_sems.at[2], bank_v)
    waiting(local_sems.at[3], blocks("q", 4))
    waiting(local_sems.at[4], bank.at[0])

    def pair_row(ref, d):
        z_at = lax.rem(z + NZ - d, NZ)
        parts = [ref[pl.ds(x_at * (2 * NZ) + z_at * 2 + core, 1), :] for x_at in (xl, 1 - xl)]
        return jnp.concatenate(parts, axis=1)

    def wide(ref):
        part = ref[...]
        return jnp.concatenate([part, part], axis=1)

    def keep_pair(d):
        keep = (wide(id_c) != pair_row(idf, d)) & (wide(req_c) != pair_row(reqf, d))
        if d == 0:
            keep = keep | (iota((2 * ROWS, 2 * ROWS), 0) == iota((2 * ROWS, 2 * ROWS), 1)) & (
                iota((2 * ROWS, 2 * ROWS), 0) < ROWS
            )
        return keep

    def both(ref):
        return ref[...].reshape(2 * ROWS, DIM)

    def pair(ref, d):
        return ref[2 * d : 2 * d + 2].reshape(2 * ROWS, DIM)

    def row_block(d):
        have("p", d)
        s = TEMP * nt(both(q_chip), pair(p_all, d)) + pair_row(shf, d)
        s = jnp.where(keep_pair(d), s, NEG)
        s_ref[d] = s
        top = jnp.maximum(s[:, :ROWS], s[:, ROWS:])
        mx_ref[...] = top if d == 0 else jnp.maximum(mx_ref[...], top)

    def col_block(d):
        have("q", d)
        t = TEMP * nt(both(p_chip), pair(q_all, d)) + wide(sh_c)
        t_ref[d] = jnp.where(keep_pair(d), t, NEG)

    pl.when(z < 2)(lambda: side("p", 7, 6))
    pl.when(z >= 2)(lambda: side("p", 1, 2))
    second("p")
    y_first(1)
    y_first(3)
    z_first("q", 0, (2, -2, 1, -1))
    x_first("q")
    x_send("q", 0)
    pl.when(z < 2)(lambda: side("p", 1, 2))
    pl.when(z >= 2)(lambda: side("p", 7, 6))
    y_relay(0)
    y_first(2)
    cut_relay("p")
    got("chip", q_chip)
    pl.when(z >= 6)(requests)
    row_block(0)
    second("q")
    x_pass("p", 3, 5, 4)
    row_block(1)
    row_block(7)
    y_relay(1)
    y_relay(3)
    row_block(2)
    row_block(6)
    side("q", 1, 2)
    side("q", 7, 6)
    y_relay(2)
    row_block(3)
    row_block(5)
    got("bank", bank.at[pl.ds(0, 5 * NH)])
    q_own = q_chip[0]
    bank_max = None
    for k in range(BANK // ROWS):
        items = bank[4 * k : 4 * k + 4].reshape(ROWS, DIM)
        at = pl.ds(k, 1)
        shift = -bank_v[1, at, :].astype(F32) * UNIT
        keep = (bank_v[0, at, :].astype(F32) != id_c[:ROWS, :]) & (bank_v[2, at, :] < AGE_LIMIT)
        s = jnp.where(keep, TEMP * nt(q_own, items) + shift, NEG)
        sm_ref[k] = s
        bank_max = s if k == 0 else jnp.maximum(bank_max, s)
    max_m = jnp.maximum(jnp.max(bank_max, axis=1, keepdims=True), FLOOR)
    lane_sum = jnp.zeros((ROWS, ROWS), F32)
    for k in range(BANK // ROWS):
        e = jnp.exp(sm_ref[k] - max_m)
        lane_sum = lane_sum + e
        em_ref[:, k * ROWS : (k + 1) * ROWS] = e.astype(BF)
    max_c, sum_c = as_row(max_m), as_row(jnp.sum(lane_sum, axis=1, keepdims=True))

    row_block(4)

    row_max = jnp.maximum(jnp.max(mx_ref[...], axis=1, keepdims=True), FLOOR)
    lane_sum = jnp.zeros((2 * ROWS, ROWS), F32)
    for d in range(NZ):
        e = jnp.exp(s_ref[d] - row_max)
        lane_sum = lane_sum + e[:, :ROWS] + e[:, ROWS:]
        e_ref[d] = e.astype(BF)
    row_sum = jnp.sum(lane_sum, axis=1, keepdims=True)
    max_a, sum_a = as_row(row_max[:ROWS]), as_row(row_sum[:ROWS])
    max_p, sum_p = as_row(row_max[ROWS:]), as_row(row_sum[ROWS:])
    stat_out[...] = jnp.where(iota((8, ROWS), 0) == 0, max_p, sum_p)
    send("stat", "stat", stat_out, stat_in, c_dev)

    got("stat", stat_in)
    max_b, sum_b = stat_in[0:1, :], stat_in[1:2, :]
    top = jnp.maximum(jnp.maximum(max_a, max_b), max_c)
    total = sum_a * jnp.exp(max_a - top) + sum_b * jnp.exp(max_b - top) + sum_c * jnp.exp(max_c - top)
    lse = top + jnp.log(total)
    lse_all[0] = jnp.broadcast_to(lse, (8, ROWS))
    for d in (4, 3, 5, 2, 6, 1, 7, 0):
        for col in (1, 0):
            if (col, d) != (0, 0):
                device = on_batch(xl if col == 0 else 1 - xl, lax.rem(z + d, NZ), core)
                send("lse", ("lse", d in (3, 4, 5)), lse_all.at[0], lse_all.at[2 * d + col], device)

    cut_relay("q")
    x_pass("q", 3, 5, 4)
    for d in range(NZ):
        part = nn(e_ref[d], pair(p_all, d))
        q_acc[...] = part if d == 0 else q_acc[...] + part
    half_out[...] = q_acc[ROWS:, :]
    send("half", "half", half_out, half_in, c_dev)
    mem_part = nn(em_ref[...], bank[...].reshape(BANK, DIM))

    for d in (0, 1, 7, 2, 6, 3, 5, 4):
        col_block(d)

    for d in (0, 1, 7, 2, 6, 3, 5, 4):
        if d == 0:
            got(("lse", False), lse_all.at[pl.ds(0, 9)])
        if d == 3:
            got(("lse", True), lse_all.at[pl.ds(0, 6)])
        level = jnp.concatenate([lse_all[2 * d][0:1, :], lse_all[2 * d + 1][0:1, :]], axis=1)
        coef = (jnp.exp(t_ref[d] - level) * pair_row(wf, d)).astype(BF)
        part = nn(coef, pair(q_all, d))
        p_acc[...] = part if d == 0 else p_acc[...] + part
    col_out[...] = p_acc[ROWS:, :]
    send("col", "col", col_out, col_in, c_dev)

    weight = wf[pl.ds(b, 1), :]
    scale = TEMP * weight
    fact_a = as_rows(scale * jnp.exp(max_a - lse))[:, 0:1]
    fact_b = as_rows(scale * jnp.exp(max_b - lse))[:, 0:1]
    fact_c = as_rows(scale * jnp.exp(max_c - lse))[:, 0:1]
    own_term = as_rows(scale)[:, 0:1]
    q_f, p_f = q_chip[0].astype(F32), p_chip[0].astype(F32)
    got("half", half_in)
    qgrad_out[...] = (
        fact_a * q_acc[:ROWS, :] + fact_b * half_in[...] + fact_c * mem_part - own_term * p_f
    )
    own_logit = TEMP * as_row(jnp.sum(q_f * p_f, axis=1, keepdims=True)) + shf[pl.ds(b, 1), :]
    loss_out[...] = lse - own_logit
    got("col", col_in)
    pgrad_out[...] = TEMP * (p_acc[:ROWS, :] + col_in[...]) - own_term * q_f

    assert (len(send_at), len(arrive_at)) == (SENDS, ARRIVALS)
    for out, ref in (
        ("p", blocks("p", 15)), ("q", blocks("q", 15)), ("bank", bank.at[pl.ds(0, 31)]),
        ("lse", lse_all.at[pl.ds(0, 15)]), ("chip", q_chip), ("stat", stat_out), ("half", half_out),
        ("col", col_out),
    ):
        sent(out, ref)


def hand_over(loss_in, qgrad_in, pgrad_in, loss_out, qgrad_out, pgrad_out):
    loss_out[...] = loss_in[...]
    qgrad_out[...] = qgrad_in[...]
    pgrad_out[...] = pgrad_in[...]


def body(queries, positives, pos_ids, pos_logq, mem_items, mem_ids, mem_logq, mem_age, counts):
    def lines(array):
        return array.reshape(-1, ROWS)

    any_spec = pl.BlockSpec(memory_space=pltpu.HBM)
    vmem_spec = pl.BlockSpec(memory_space=pltpu.VMEM)
    vmem = pltpu.VMEM
    scratch = [
        vmem((2 * NZ, ROWS, DIM), BF),
        vmem((2 * NZ, ROWS, DIM), BF),
        vmem((2, ROWS, DIM), BF),
        vmem((2, ROWS, DIM), BF),
        vmem((BLOCKS, SLOTS, DIM), BF),
        vmem((NZ, 2 * ROWS, 2 * ROWS), F32),
        vmem((NZ, 2 * ROWS, 2 * ROWS), F32),
        vmem((NZ, 2 * ROWS, 2 * ROWS), BF),
        vmem((2 * ROWS, ROWS), F32),
        vmem((ROWS, ROWS), jnp.int32),
        vmem((2, BLOCKS, ROWS), jnp.int32),
        vmem((3, 8, ROWS), jnp.int32),
        vmem((ROWS, ROWS), F32),
        vmem((ROWS, ROWS), F32),
        vmem((ROWS, ROWS), F32),
        vmem((BLOCKS, ROWS), F32),
        vmem((BLOCKS, ROWS), F32),
        vmem((BLOCKS, ROWS), F32),
        vmem((BLOCKS, ROWS), F32),
        vmem((2 * ROWS, ROWS), F32),
        vmem((2 * ROWS, ROWS), F32),
        vmem((2 * ROWS, ROWS), F32),
        vmem((8, ROWS), F32),
        vmem((8, ROWS), F32),
        vmem((2 * NZ, 8, ROWS), F32),
        vmem((ROWS, DIM), F32),
        vmem((ROWS, DIM), F32),
        vmem((ROWS, DIM), F32),
        vmem((ROWS, DIM), F32),
        vmem((2 * ROWS, DIM), F32),
        vmem((2 * ROWS, DIM), F32),
        vmem((BANK // ROWS, ROWS, ROWS), F32),
        vmem((ROWS, BANK), BF),
        pltpu.SemaphoreType.DMA((SENDS,)),
        pltpu.SemaphoreType.DMA((ARRIVALS,)),
        pltpu.SemaphoreType.DMA((LOADS,)),
    ]
    loss, query_grad, positive_grad = pl.pallas_call(
        kernel,
        out_shape=(
            jax.ShapeDtypeStruct((1, ROWS), F32),
            jax.ShapeDtypeStruct((ROWS, DIM), F32),
            jax.ShapeDtypeStruct((ROWS, DIM), F32),
        ),
        in_specs=[any_spec] * 9,
        out_specs=(vmem_spec, vmem_spec, vmem_spec),
        scratch_shapes=scratch,
        compiler_params=pltpu.CompilerParams(
            collective_id=0, has_side_effects=True, vmem_limit_bytes=67043328
        ),
        name="retrieval",
    )(
        queries, positives, mem_items, lines(counts), lines(pos_ids), lines(pos_logq),
        lines(mem_ids), lines(mem_logq), lines(mem_age),
    )
    loss, query_grad, positive_grad = pl.pallas_call(
        hand_over,
        out_shape=(
            jax.ShapeDtypeStruct((1, ROWS), F32),
            jax.ShapeDtypeStruct((ROWS, DIM), F32),
            jax.ShapeDtypeStruct((ROWS, DIM), F32),
        ),
        in_specs=[vmem_spec] * 3,
        out_specs=(vmem_spec, vmem_spec, vmem_spec),
        name="results",
    )(loss, query_grad, positive_grad)
    return loss.reshape(ROWS), query_grad, positive_grad


def solution(mesh):
    in_specs = (
        P(("mem", "batch"), None),
        P(("mem", "batch"), None),
        P(),
        P(),
        P(("batch", "mem"), None),
        P(),
        P(),
        P(),
        P(),
    )
    out_specs = (P(("mem", "batch")), P(("mem", "batch"), None), P(("mem", "batch"), None))
    return jax.shard_map(body, mesh=mesh, in_specs=in_specs, out_specs=out_specs, check_vma=False)
```
